32 devices in a mesh: user: 8 (over z, x), item: 4 (over y, core).
Axes of the slice: x: 2, y: 2, z: 4, core: 2. Of those that a mesh axis runs over, the one named last changes fastest.
Arguments:
- ratings: bfloat16 [32768, 8192], P('user', 'item'), may hold values from -6 to 6
- tile_mask: int32 [128, 32], P('user', 'item'), may hold values 0 or 1
- user_factors: bfloat16 [128, 256, 128], P('user', 'item'), may hold values from -1.796875 to 1.796875
- item_factors: bfloat16 [8192, 128], P('item'), may hold values from -1.796875 to 1.796875
- neighbours: int32 [128, 4], replicated, may hold values from 0 to 127, as said below
- edge_weight: float32 [128, 4], replicated, may hold values from 0.5 to 8
- dual: float32 [128, 4, 256, 128], P('user', None, 'item'), may hold values from -1.8 to 1.8
Outputs:
- user_update: float32 [128, 256, 128], P('user', 'item')
- dual_update: float32 [128, 4, 256, 128], P('user', None, 'item')
- item_gradient: float32 [8192, 128], P('item')
The draws below stay inside these ranges and needn't reach their ends.
Inputs may be any that keep to these rules, and one draw needn't show every extreme that they name: `neighbours`: among the 64 entries of rows d * 16 to (d + 1) * 16 - 1, for any d, at most 16 name blocks of one group c * 16 to (c + 1) * 16 - 1, and some group is named exactly 16 times.
All inputs are finite; a program needn't handle non-finite values. No bound on the sum of `tile_mask` on one device may be relied on, other than what follows from the above.
Results may differ from the reference program's by a relative error of at most 0.0012.
Values may be sent and summed in bfloat16 or wider, within the bound.
A program may use at most 128 MiB of HBM per device.

```python
import math
import jax
import jax.numpy as jnp
from jax import lax

R = 128
BROWS = 256
K = 4
ITILE = 256
ITERS = 2
BLK_DEV = 16
BLOCKS = 128
USERS = 32768
ITEMS = 8192
CAP = 16
N_USER = 8


def draw_neighbours(key, part):
    edges_per = BLK_DEV * K

    def one_device(device_key):
        key_main, key_rest, key_order, key_block = jax.random.split(device_key, 4)
        main_owner = jax.random.randint(key_main, (), 0, N_USER)
        spread = (main_owner + 1 + jnp.arange((N_USER - 1) * CAP) // CAP) % N_USER
        spread = jax.random.permutation(key_rest, spread)[:edges_per - CAP]
        owners = jnp.concatenate([jnp.full((CAP,), main_owner, jnp.int32), spread.astype(jnp.int32)])
        owners = jax.random.permutation(key_order, owners)
        within = jax.random.randint(key_block, (edges_per,), 0, BLK_DEV)
        return (owners * BLK_DEV + within).astype(jnp.int32)
    device_keys = jax.random.split(jax.random.fold_in(key, 7), N_USER)
    return jax.vmap(one_device)(device_keys).reshape(BLOCKS, K)


def set_ends(result, key, least, high):
    index_at = [jax.random.randint(jax.random.fold_in(key, axis), (), 0, length) for axis, length in enumerate(result.shape)]
    widest = result.shape.index(max(result.shape))
    beside = index_at[:widest] + [(index_at[widest] + 1) % result.shape[widest]] + index_at[widest + 1:]
    return result.at[tuple(index_at)].set(least).at[tuple(beside)].set(high)


def level_of(own_key, extent, shards, low, high):
    loudness = 1.0
    for dim, parts in shards:
        steps = jax.random.uniform(jax.random.fold_in(jax.random.fold_in(own_key, 6), dim), (parts,), jnp.float32, low / len(shards), high / len(shards))
        loudness = loudness * jnp.repeat(jnp.exp(steps), extent[dim] // parts).reshape((-1,) + (1,) * (len(extent) - 1 - dim))
    return loudness


def noise(stream_key, dims, deviation, limit, pieces=(), kind=jnp.bfloat16):
    factor_of = level_of(stream_key, dims, pieces, -0.22, 0.18) if pieces else 1.0
    drawn = jax.random.normal(stream_key, dims, jnp.float32) * deviation * factor_of
    return jnp.minimum(jnp.maximum(drawn, -limit), limit).astype(kind)


def setup_inputs(seed: int = 0) -> dict:
    keys = jax.random.split(jax.random.key(seed), 8)
    ratings = noise(keys[0], (USERS, ITEMS), 1.0, 6.0, ((0, 8), (1, 4)))
    tile_mask = set_ends((jax.random.randint(keys[1], (BLOCKS, ITEMS // ITILE), 0, 2) < 1).astype(jnp.int32), jax.random.fold_in(keys[1], 1), 0, 1)
    user_factors = noise(keys[2], (BLOCKS, BROWS, R), 0.3, 1.796875, ((0, 8), (1, 4)))
    item_factors = noise(keys[3], (ITEMS, R), 0.3, 1.796875, ((0, 4),))
    neighbours = draw_neighbours(jax.random.fold_in(keys[7], 71), 0)
    edge_weight = jnp.clip(jnp.exp(jax.random.uniform(keys[5], (BLOCKS, K), jnp.float32, math.log(0.5), math.log(8.0))), 0.5, 8.0)
    dual = noise(keys[6], (BLOCKS, K, BROWS, R), 0.3, 1.8, ((0, 8), (2, 4)), jnp.float32)
    return dict(ratings=ratings, tile_mask=tile_mask, user_factors=user_factors, item_factors=item_factors, neighbours=neighbours, edge_weight=edge_weight, dual=dual)


descent = 0.5
dual_step = 0.5
primal_step = 0.25

def reference(ratings, tile_mask, user_factors, item_factors, neighbours, edge_weight, dual):
    rating_blocks = ratings.reshape(BLOCKS, BROWS, ITEMS)

    def one_block(carry, inputs):
        users_block, rating_block, tile_row = inputs
        scores = jnp.dot(users_block, item_factors.T, preferred_element_type=jnp.float32)
        observed = jnp.repeat(tile_row.astype(jnp.float32), ITILE)[None, :]
        errors = (observed * (scores - rating_block.astype(jnp.float32))).astype(jnp.bfloat16)
        user_term = jnp.dot(errors, item_factors, preferred_element_type=jnp.float32)
        item_term = jnp.dot(errors.T, users_block, preferred_element_type=jnp.float32)
        return (carry + item_term, user_term)
    item_part, user_part = lax.scan(one_block, jnp.zeros((ITEMS, R), jnp.float32), (user_factors, rating_blocks, tile_mask))
    item_gradient = item_part / math.sqrt(USERS)
    user_grad = user_part / math.sqrt(ITEMS)
    target = user_factors.astype(jnp.float32) - descent * user_grad
    targets_flat = neighbours.reshape(-1).astype(jnp.int32)
    radius = edge_weight.reshape(-1)[:, None]
    primal = target
    extra = target
    flux = dual.reshape(BLOCKS * K, BROWS, R)
    for sweep in range(ITERS):
        moved = flux + dual_step * (jnp.repeat(extra, K, axis=0) - extra[targets_flat])
        length = jnp.sqrt(lax.optimization_barrier(jnp.sum(moved * moved, axis=-1)))
        flux = moved * (radius / jnp.maximum(length, radius))[..., None]
        inflow = jax.ops.segment_sum(flux, targets_flat, num_segments=BLOCKS)
        divergence = lax.optimization_barrier(jnp.sum(flux.reshape(BLOCKS, K, BROWS, R), axis=1)) - inflow
        newer = (primal - primal_step * divergence + primal_step * target) / (1.0 + primal_step)
        extra = 2.0 * newer - primal
        primal = newer
    return (primal, flux.reshape(BLOCKS, K, BROWS, R), item_gradient)
```

```python
import functools
import math

import jax
import jax.numpy as jnp
from jax import lax
from jax.experimental import pallas as pl
from jax.experimental.pallas import tpu as pltpu
from jax.sharding import PartitionSpec as P

ITERS = 2
TOP = 32767.0
TINY = 1e-30
CHUNKS = 4
SLOTS = 3
MESH = pl.DeviceIdType.MESH

descent = 0.5
dual_step = 0.5
primal_step = 0.25


def flip(index, mask, size):
    out, bit = 0, 1
    while bit < size:
        out = out + bit * lax.rem(index // bit + mask // bit, 2)
        bit *= 2
    return out


def tiles(x):
    return x.reshape(x.shape[0] // 8, 8, x.shape[1])


def peak(x):
    return jnp.max(jnp.abs(tiles(x)), axis=0)


def coded(x, inverse):
    y = tiles(x) * inverse[None]
    return jnp.round(y).astype(jnp.int32).astype(jnp.int16).reshape(x.shape)


def plain(q, scale):
    y = q.astype(jnp.int32).astype(jnp.float32)
    return (tiles(y) * scale[None]).reshape(q.shape)


def steps_of(top):
    top = jnp.maximum(top, TINY)
    return TOP / top, top * (1.0 / TOP)


def kernel(
    dims, rating_ref, seen_ref, user_ref, item_ref, dual_ref, diff_ref, back_ref, weight_ref,
    out_p, out_d, out_i,
    rat, gat, own_part, total, snd_u, snd_us, rec_u, rec_us,
    snd_d, snd_ds, rec_d, rec_ds, tgt, snd_t, snd_ts, rec_t, rec_ts,
    xs, ex, hl, fl, fhl, snd_r, snd_rs, rec_r, rec_rs,
    ired, snd_i, snd_is, rec_i, rec_is, gi, gis,
    rat_m, ag_s, ag_r, u_s, u_r, us_s, us_r, d_s, d_r, ds_s, ds_r, t_s, t_r, ts_s, ts_r,
    r_s, r_r, rs_s, rs_r, i_s, i_r, is_s, is_r, a_s, a_r, as_s, as_r,
):
    NU, NI, B, S, K, C, W = dims
    T = S // NU
    E = B * K
    NB = B * NU
    EE = E * NU
    LOG = NU.bit_length() - 1
    PART = B // CHUNKS
    ROWS = PART * S
    STEPS = NI * CHUNKS
    PAIR = 2 if T % 2 == 0 else 1
    user_scale = 1.0 / math.sqrt(C * NI)
    item_scale = 1.0 / math.sqrt(B * S * NI * NU)

    u = lax.axis_index("user")
    i = lax.axis_index("item")

    def send(src, dst, s, r, device):
        return pltpu.make_async_remote_copy(
            src_ref=src, dst_ref=dst, send_sem=s, recv_sem=r, device_id=device, device_id_type=MESH
        )

    def along(d):
        return lax.rem(u + d, NU)

    def behind(d):
        return lax.rem(u + NU - d, NU)

    barrier = pltpu.get_barrier_semaphore()
    for d in range(1, NU):
        pl.semaphore_signal(barrier, inc=1, device_id=(along(d), i), device_id_type=MESH)
    for q in range(1, NI):
        pl.semaphore_signal(barrier, inc=1, device_id=(u, flip(i, q, NI)), device_id_type=MESH)

    def place(s):
        p = s // CHUNKS
        c = lax.rem(s, CHUNKS)
        q = lax.rem(NI - p, NI)
        return p, c, q, flip(i, q, NI)

    def fetch(s):
        _, c, _, j = place(s)
        slot = lax.rem(s, SLOTS)
        return pltpu.make_async_copy(
            rating_ref.at[pl.ds(c * PART, PART), j], rat.at[slot], rat_m.at[slot]
        )

    for s in range(SLOTS - 1):
        fetch(jnp.int32(s)).start()

    def gather(q, c):
        rows = pl.ds(pl.multiple_of(c * ROWS, ROWS), ROWS)
        return send(
            user_ref.at[rows], gat.at[q, rows], ag_s.at[q, c], ag_r.at[q, c], (u, flip(i, q, NI))
        )

    def give_user(q, c):
        device = (u, flip(i, q, NI))
        return (
            send(snd_u.at[q, c], rec_u.at[q, c], u_s.at[q, c], u_r.at[q, c], device),
            send(snd_us.at[q, c], rec_us.at[q, c], us_s.at[q, c], us_r.at[q, c], device),
        )

    def gradient(early, s, _):
        p, c, q, j = place(s)
        slot = lax.rem(s, SLOTS)

        @pl.when(s + SLOTS - 1 < STEPS)
        def _():
            fetch(s + SLOTS - 1).start()

        fetch(s).wait()

        if not early:
            @pl.when(p > 0)
            def _():
                gather(q, c).wait_recv()

        users = gat[q, pl.ds(pl.multiple_of(c * ROWS, ROWS), ROWS)]
        items = item_ref[...]
        scores = lax.dot_general(
            users, items, (((1,), (1,)), ((), ())), preferred_element_type=jnp.float32
        )
        error = scores.reshape(PART, S, C) - rat[slot].astype(jnp.float32)
        error = (seen_ref[pl.ds(c * PART, PART)] * error).astype(jnp.bfloat16).reshape(ROWS, C)
        term = jnp.dot(error, items, preferred_element_type=jnp.float32)
        total[...] += jnp.dot(users.T, error, preferred_element_type=jnp.float32)

        if early:
            own_part[c] = term
            return 0

        @pl.when(p == 0)
        def _():
            own_part[c] = term

        @pl.when(p > 0)
        def _():
            inverse, scale = steps_of(peak(term))
            snd_u[q, c] = coded(term, inverse)
            snd_us[q, c] = scale
            for copy in give_user(q, c):
                copy.start()

        return 0

    top = lax.fori_loop(
        0, EE * S // (NU * 64),
        lambda k, m: jnp.maximum(m, peak(dual_ref[pl.ds(pl.multiple_of(k * 64, 64), 64)])),
        jnp.zeros((8, W), jnp.float32),
    )
    dual_inverse, dual_scale = steps_of(jnp.max(top, axis=0, keepdims=True))
    snd_ds[...] = dual_scale

    def turn_dual(r, _):
        snd_d[r] = coded(dual_ref[pl.ds(r, E, stride=S), :], dual_inverse)
        return 0

    lax.fori_loop(0, S, turn_dual, 0, unroll=4)

    gat[0] = user_ref[...]
    total[...] = jnp.zeros_like(total)
    lax.fori_loop(0, 2, functools.partial(gradient, True), 0)

    pl.semaphore_wait(barrier, NU - 1 + NI - 1)

    for q in range(NI - 1, 0, -1):
        for c in range(CHUNKS):
            gather(q, c).start()

    def give_dual(d):
        device = (along(d), i)
        return (
            send(snd_d.at[pl.ds(along(d) * T, T)], rec_d.at[u], d_s.at[d], d_r.at[d], device),
            send(snd_ds, rec_ds.at[u], ds_s.at[d], ds_r.at[d], device),
        )

    for d in range(1, NU):
        for copy in give_dual(d):
            copy.start()
    rec_d[u] = snd_d[pl.ds(u * T, T)]
    rec_ds[u] = dual_scale

    lax.fori_loop(2, STEPS, functools.partial(gradient, False), 0)

    def half(s):
        h = C >> (s + 1)
        base = 0
        for t in range(s):
            base = base + lax.rem(u // (1 << t), 2) * (C >> (t + 1))
        bit = lax.rem(u // (1 << s), 2)
        keep = pl.ds(pl.multiple_of(base + bit * h, h), h)
        away = pl.ds(pl.multiple_of(base + (1 - bit) * h, h), h)
        return keep, away, h

    def partner(s):
        return (flip(u, 1 << s, NU), i)

    def give_item(s):
        h = C >> (s + 1)
        return (
            send(snd_i.at[s, pl.ds(0, h)], rec_i.at[s, pl.ds(0, h)], i_s.at[s], i_r.at[s], partner(s)),
            send(snd_is.at[s], rec_is.at[s], is_s.at[s], is_r.at[s], partner(s)),
        )

    def halve_send(s):
        _, away, h = half(s)
        part = ired[away]
        inverse, scale = steps_of(peak(part))
        snd_i[s, pl.ds(0, h)] = coded(part, inverse)
        snd_is[s] = scale
        for copy in give_item(s):
            copy.start()

    def halve_take(s):
        keep, _, h = half(s)
        for copy in give_item(s):
            copy.wait_recv()
        ired[keep] += plain(rec_i[s, pl.ds(0, h)], rec_is[s])

    SEG = C // NU

    def give_all(s):
        keep, _, h = half(s)
        n = h // SEG
        base = 0
        for t in range(s + 1):
            base = base + lax.rem(u // (1 << t), 2) * ((C >> (t + 1)) // SEG)
        tile = pl.ds(base, n)
        return (
            send(gi.at[keep], gi.at[keep], a_s.at[s], a_r.at[s], partner(s)),
            send(gis.at[tile], gis.at[tile], as_s.at[s], as_r.at[s], partner(s)),
        )

    def double_first():
        keep, _, _ = half(LOG - 1)
        base = 0
        for t in range(LOG):
            base = base + lax.rem(u // (1 << t), 2) * (NU >> (t + 1))
        part = ired[keep]
        inverse, scale = steps_of(peak(part))
        gi[keep] = coded(part, inverse)
        gis[base] = scale

    def double_send(s):
        for copy in give_all(s):
            copy.start()

    def double_take(s):
        for copy in give_all(s):
            copy.wait_recv()

    ired[...] = total[...].T * item_scale
    halve_send(0)

    def close(c, m):
        g = own_part[c]
        for q in range(NI - 1, 0, -1):
            for copy in give_user(q, c):
                copy.wait_recv()
            g = g + plain(rec_u[q, c], rec_us[q, c])
        rows = pl.ds(pl.multiple_of(c * ROWS, ROWS), ROWS)
        t = user_ref[rows].astype(jnp.float32) - (descent * user_scale) * g
        tgt[rows] = t
        return jnp.maximum(m, peak(t))

    top = lax.fori_loop(0, CHUNKS, close, jnp.zeros((8, W), jnp.float32))
    target_inverse, target_scale = steps_of(jnp.max(top, axis=0, keepdims=True))
    snd_ts[...] = target_scale

    def turn_target(r, _):
        snd_t[r] = coded(tgt[pl.ds(r, B, stride=S), :], target_inverse)
        return 0

    lax.fori_loop(0, S, turn_target, 0, unroll=4)

    def give_target(d):
        device = (along(d), i)
        return (
            send(snd_t.at[pl.ds(along(d) * T, T)], rec_t.at[u], t_s.at[d], t_r.at[d], device),
            send(snd_ts, rec_ts.at[u], ts_s.at[d], ts_r.at[d], device),
        )

    for d in range(1, NU):
        for copy in give_target(d):
            copy.start()
    rec_t[u] = snd_t[pl.ds(u * T, T)]
    rec_ts[u] = target_scale

    halve_take(0)
    halve_send(1)

    for d in range(1, NU):
        for copy in give_dual(d):
            copy.wait_recv()
    for d in range(1, NU):
        for copy in give_target(d):
            copy.wait_recv()

    GROUP = 128

    def split(x):
        high = x.astype(jnp.bfloat16)
        return high, (x - high.astype(jnp.float32)).astype(jnp.bfloat16)

    def give_result(d, ch):
        device = (along(d), i)
        rows = pl.ds(ch * PAIR, PAIR)
        return (
            send(snd_r.at[along(d), rows], rec_r.at[u, rows], r_s.at[d, ch], r_r.at[d, ch], device),
            send(snd_rs.at[ch], rec_rs.at[u, ch], rs_s.at[d, ch], rs_r.at[d, ch], device),
        )

    def fold(m):
        m = jnp.max(m, axis=0, keepdims=True)
        out = m[:, :W]
        for n in range(1, PAIR):
            out = jnp.maximum(out, m[:, n * W : (n + 1) * W])
        return out

    def sweep_rows(ch, _):
        for n in range(PAIR):
            r = ch * PAIR + n
            lanes = slice(n * W, (n + 1) * W)
            for v in range(NU):
                xs[v * B : (v + 1) * B, lanes] = plain(rec_t[v, r], rec_ts[v])
                fl[v * E : (v + 1) * E, lanes] = plain(rec_d[v, r], rec_ds[v])

        peaks = None
        for sweep in range(ITERS):
            source = xs[...] if sweep == 0 else ex[...]
            hl[:NB], hl[NB:] = split(source)
            peaks = jnp.zeros((8, PAIR * W), jnp.float32)
            for g in range(0, EE, GROUP):
                rows = slice(g, g + GROUP)
                slope = jnp.dot(diff_ref[rows], hl[...], preferred_element_type=jnp.float32)
                moved = fl[rows] + dual_step * slope
                w = weight_ref[rows]
                parts = []
                for n in range(PAIR):
                    m = moved[:, n * W : (n + 1) * W]
                    square = jnp.sum(m * m, axis=-1, keepdims=True)
                    parts.append(m * (w * lax.rsqrt(jnp.maximum(square, w * w))))
                flux = jnp.concatenate(parts, axis=1) if PAIR > 1 else parts[0]
                fl[rows] = flux
                fhl[rows], fhl[EE + g : EE + g + GROUP] = split(flux)
                peaks = jnp.maximum(peaks, peak(flux))
            div = jnp.dot(back_ref[...], fhl[...], preferred_element_type=jnp.float32)
            target = xs[...]
            if sweep == 0:
                primal = target
            newer = (primal - primal_step * div + primal_step * target) / (1.0 + primal_step)
            if sweep < ITERS - 1:
                ex[...] = 2.0 * newer - primal
            primal = newer

        flux_inverse, flux_scale = steps_of(fold(peaks))
        primal_inverse, primal_scale = steps_of(fold(peak(primal)))
        scales = jnp.concatenate([flux_scale, primal_scale], axis=0)
        snd_rs[ch] = scales
        for n in range(PAIR):
            r = ch * PAIR + n
            lanes = slice(n * W, (n + 1) * W)
            for v in range(NU):
                snd_r[v, r, :E] = coded(fl[v * E : (v + 1) * E, lanes], flux_inverse)
                snd_r[v, r, E:] = coded(primal[v * B : (v + 1) * B, lanes], primal_inverse)
        for d in range(1, NU):
            for copy in give_result(d, ch):
                copy.start()
        rows = pl.ds(ch * PAIR, PAIR)
        rec_r[u, rows] = snd_r[u, rows]
        rec_rs[u, ch] = scales
        return 0

    PARTS = T // PAIR
    lax.fori_loop(0, PARTS, sweep_rows, 0)

    for s in range(1, LOG):
        halve_take(s)
        if s < LOG - 1:
            halve_send(s + 1)
    double_first()
    double_send(LOG - 1)

    def place_rows(v, ch):
        scales = rec_rs[v, ch]
        for n in range(PAIR):
            r = ch * PAIR + n
            row = v * T + r
            out_d[pl.ds(row, E, stride=S), :] = plain(rec_r[v, r, :E], scales[0:1])
            out_p[pl.ds(row, B, stride=S), :] = plain(rec_r[v, r, E:], scales[1:2])

    def finish(ch, _):
        place_rows(u, ch)
        for d in range(1, NU):
            for copy in give_result(d, ch):
                copy.wait_recv()
            place_rows(behind(d), ch)
        return 0

    for s in range(LOG - 1, 0, -1):
        double_take(s)
        double_send(s - 1)
    lax.fori_loop(0, PARTS, finish, 0)
    double_take(0)
    for seg in range(NU):
        rows = slice(seg * SEG, (seg + 1) * SEG)
        out_i[rows] = plain(gi[rows], gis[seg])

    for q in range(1, NI):
        for c in range(CHUNKS):
            gather(q, c).wait_send()
            for copy in give_user(q, c):
                copy.wait_send()
    for d in range(1, NU):
        for copy in give_dual(d) + give_target(d):
            copy.wait_send()
        for ch in range(PARTS):
            for copy in give_result(d, ch):
                copy.wait_send()
    for s in range(LOG):
        for copy in give_item(s) + give_all(s):
            copy.wait_send()


def shards(ratings, tile_mask, user_factors, item_factors, neighbours, edge_weight, dual):
    B, S, W = user_factors.shape
    K = neighbours.shape[1]
    NU = lax.axis_size("user")
    NI = lax.axis_size("item")
    C = item_factors.shape[0]
    T = S // NU
    E = B * K
    NB = B * NU
    EE = E * NU
    LOG = NU.bit_length() - 1
    ROWS = B // CHUNKS * S
    PAIR = 2 if T % 2 == 0 else 1
    PARTS = T // PAIR

    near = neighbours.reshape(-1)
    blocks = jnp.arange(NB, dtype=jnp.int32)
    home = jnp.arange(EE, dtype=jnp.int32) // K

    def hit(a, b):
        return (a == b).astype(jnp.bfloat16)

    diff = hit(home[:, None], blocks[None]) - hit(near[:, None], blocks[None])
    back = hit(blocks[:, None], home[None]) - hit(blocks[:, None], near[None])
    diff = jnp.concatenate([diff, diff], axis=1)
    back = jnp.concatenate([back, back], axis=1)
    weight = jnp.broadcast_to(edge_weight.reshape(-1)[:, None], (EE, W))
    seen = jnp.repeat(tile_mask.astype(jnp.float32), C // tile_mask.shape[1], axis=1)[:, None, :]

    f32, i16, bf16 = jnp.float32, jnp.int16, jnp.bfloat16
    V = pltpu.VMEM
    dma = pltpu.SemaphoreType.DMA
    vmem = pl.BlockSpec(memory_space=pltpu.VMEM)
    scratch = [
        V((SLOTS, B // CHUNKS, S, C), bf16), V((NI, B * S, W), bf16), V((CHUNKS, ROWS, W), f32),
        V((W, C), f32),
        V((NI, CHUNKS, ROWS, W), i16), V((NI, CHUNKS, 8, W), f32),
        V((NI, CHUNKS, ROWS, W), i16), V((NI, CHUNKS, 8, W), f32),
        V((S, E, W), i16), V((1, W), f32), V((NU, T, E, W), i16), V((NU, 1, W), f32),
        V((B * S, W), f32), V((S, B, W), i16), V((1, W), f32), V((NU, T, B, W), i16), V((NU, 1, W), f32),
        V((NB, PAIR * W), f32), V((NB, PAIR * W), f32), V((2 * NB, PAIR * W), bf16),
        V((EE, PAIR * W), f32), V((2 * EE, PAIR * W), bf16),
        V((NU, T, E + B, W), i16), V((PARTS, 2, W), f32),
        V((NU, T, E + B, W), i16), V((NU, PARTS, 2, W), f32),
        V((C, W), f32), V((LOG, C // 2, W), i16), V((LOG, 8, W), f32),
        V((LOG, C // 2, W), i16), V((LOG, 8, W), f32), V((C, W), i16), V((NU, 8, W), f32),
        dma((SLOTS,)),
        *[dma((NI, CHUNKS)) for _ in range(6)],
        *[dma((NU,)) for _ in range(8)],
        *[dma((NU, PARTS)) for _ in range(4)],
        *[dma((LOG,)) for _ in range(8)],
    ]
    primal, flux, item_grad = pl.pallas_call(
        functools.partial(kernel, (NU, NI, B, S, K, C, W)),
        out_shape=(
            jax.ShapeDtypeStruct((B * S, W), f32),
            jax.ShapeDtypeStruct((B * K * S, W), f32),
            jax.ShapeDtypeStruct((C, W), f32),
        ),
        in_specs=[pl.BlockSpec(memory_space=pl.ANY)] + [vmem] * 7,
        out_specs=[vmem] * 3,
        scratch_shapes=scratch,
        compiler_params=pltpu.CompilerParams(
            collective_id=0, has_side_effects=True, vmem_limit_bytes=56 << 20
        ),
        cost_estimate=pl.CostEstimate(
            flops=6 * B * S * NI * C * W, bytes_accessed=2 * B * S * NI * C, transcendentals=0
        ),
    )(
        ratings.reshape(B, NI, S, C), seen, user_factors.reshape(B * S, W), item_factors,
        dual.reshape(B * K * S, W), diff, back, weight,
    )
    return (primal.reshape(B, S, W), flux.reshape(B, K, S, W), item_grad)


def solution(mesh):
    in_specs = (
        P("user", "item"),
        P("user", "item"),
        P("user", "item", None),
        P("item", None),
        P(),
        P(),
        P("user", None, "item", None),
    )
    out_specs = (P("user", "item", None), P("user", None, "item", None), P("item", None))
    return jax.shard_map(shards, mesh=mesh, in_specs=in_specs, out_specs=out_specs, check_vma=False)
```

```python
import functools
import math

import jax
import jax.numpy as jnp
from jax import lax
from jax.experimental import pallas as pl
from jax.experimental.pallas import tpu as pltpu
from jax.sharding import PartitionSpec as P

ITERS = 2
TOP = 32767.0
TINY = 1e-30
CHUNKS = 4
SLOTS = 3
MESH = pl.DeviceIdType.MESH

descent = 0.5
dual_step = 0.5
primal_step = 0.25


def flip(index, mask, size):
    out, bit = 0, 1
    while bit < size:
        out = out + bit * lax.rem(index // bit + mask // bit, 2)
        bit *= 2
    return out


def tiles(x):
    return x.reshape(x.shape[0] // 8, 8, x.shape[1])


def peak(x):
    return jnp.max(jnp.abs(tiles(x)), axis=0)


def coded(x, inverse):
    y = tiles(x) * inverse[None]
    return jnp.round(y).astype(jnp.int32).astype(jnp.int16).reshape(x.shape)


def plain(q, scale):
    y = q.astype(jnp.int32).astype(jnp.float32)
    return (tiles(y) * scale[None]).reshape(q.shape)


def steps_of(top):
    top = jnp.maximum(top, TINY)
    return TOP / top, top * (1.0 / TOP)


def kernel(
    dims, rating_ref, mask_ref, user_ref, item_ref, dual_ref, near_ref, edge_ref,
    rec_r, rec_rs, gi, gis,
    seen_ref, diff_ref, back_ref, weight_ref, rat, gat, own_part, total, snd_u, snd_us, rec_u, rec_us,
    snd_d, snd_ds, rec_d, rec_ds, tgt, snd_t, snd_ts, rec_t, rec_ts,
    xs, ex, hl, fl, fhl, snd_r, snd_rs,
    ired, snd_i, snd_is, rec_i, rec_is,
    rat_m, ag_s, ag_r, u_s, u_r, us_s, us_r, d_s, d_r, ds_s, ds_r, t_s, t_r, ts_s, ts_r,
    r_s, r_r, rs_s, rs_r, i_s, i_r, is_s, is_r, a_s, a_r, as_s, as_r,
):
    NU, NI, B, S, K, C, W = dims
    T = S // NU
    E = B * K
    NB = B * NU
    EE = E * NU
    LOG = NU.bit_length() - 1
    PART = B // CHUNKS
    ROWS = PART * S
    STEPS = NI * CHUNKS
    PAIR = 2 if T % 2 == 0 else 1
    user_scale = 1.0 / math.sqrt(C * NI)
    item_scale = 1.0 / math.sqrt(B * S * NI * NU)

    u = lax.axis_index("user")
    i = lax.axis_index("item")

    def send(src, dst, s, r, device):
        return pltpu.make_async_remote_copy(
            src_ref=src, dst_ref=dst, send_sem=s, recv_sem=r, device_id=device, device_id_type=MESH
        )

    def along(d):
        return lax.rem(u + d, NU)

    def behind(d):
        return lax.rem(u + NU - d, NU)

    barrier = pltpu.get_barrier_semaphore()
    for d in range(1, NU):
        pl.semaphore_signal(barrier, inc=1, device_id=(along(d), i), device_id_type=MESH)
    for q in range(1, NI):
        pl.semaphore_signal(barrier, inc=1, device_id=(u, flip(i, q, NI)), device_id_type=MESH)

    def place(s):
        p = s // CHUNKS
        c = lax.rem(s, CHUNKS)
        q = lax.rem(NI - p, NI)
        return p, c, q, flip(i, q, NI)

    def fetch(s):
        _, c, _, j = place(s)
        slot = lax.rem(s, SLOTS)
        return pltpu.make_async_copy(
            rating_ref.at[pl.ds(c * PART, PART), j], rat.at[slot], rat_m.at[slot]
        )

    for s in range(SLOTS - 1):
        fetch(jnp.int32(s)).start()

    def gather(q, c):
        rows = pl.ds(pl.multiple_of(c * ROWS, ROWS), ROWS)
        return send(
            user_ref.at[rows], gat.at[q, rows], ag_s.at[q, c], ag_r.at[q, c], (u, flip(i, q, NI))
        )

    def give_user(q, c):
        device = (u, flip(i, q, NI))
        return (
            send(snd_u.at[q, c], rec_u.at[q, c], u_s.at[q, c], u_r.at[q, c], device),
            send(snd_us.at[q, c], rec_us.at[q, c], us_s.at[q, c], us_r.at[q, c], device),
        )

    def gradient(early, s, _):
        p, c, q, j = place(s)
        slot = lax.rem(s, SLOTS)

        @pl.when(s + SLOTS - 1 < STEPS)
        def _():
            fetch(s + SLOTS - 1).start()

        fetch(s).wait()

        if not early:
            @pl.when(p > 0)
            def _():
                gather(q, c).wait_recv()

        users = gat[q, pl.ds(pl.multiple_of(c * ROWS, ROWS), ROWS)]
        items = item_ref[...]
        scores = lax.dot_general(
            users, items, (((1,), (1,)), ((), ())), preferred_element_type=jnp.float32
        )
        error = scores.reshape(PART, S, C) - rat[slot].astype(jnp.float32)
        error = (seen_ref[pl.ds(c * PART, PART)] * error).astype(jnp.bfloat16).reshape(ROWS, C)
        term = jnp.dot(error, items, preferred_element_type=jnp.float32)
        total[...] += jnp.dot(users.T, error, preferred_element_type=jnp.float32)

        if early:
            own_part[c] = term
            return 0

        @pl.when(p == 0)
        def _():
            own_part[c] = term

        @pl.when(p > 0)
        def _():
            inverse, scale = steps_of(peak(term))
            snd_u[q, c] = coded(term, inverse)
            snd_us[q, c] = scale
            for copy in give_user(q, c):
                copy.start()

        return 0

    top = lax.fori_loop(
        0, EE * S // (NU * 64),
        lambda k, m: jnp.maximum(m, peak(dual_ref[pl.ds(pl.multiple_of(k * 64, 64), 64)])),
        jnp.zeros((8, W), jnp.float32),
    )
    dual_inverse, dual_scale = steps_of(jnp.max(top, axis=0, keepdims=True))
    snd_ds[...] = dual_scale

    def turn_dual(r, _):
        for k in range(K):
            part = dual_ref[pl.ds(k * S + r, B, stride=K * S), :]
            snd_d[r, k * B : (k + 1) * B] = coded(part, dual_inverse)
        return 0

    lax.fori_loop(0, S, turn_dual, 0, unroll=4)

    tile = C // mask_ref.shape[0]

    def fill(b, _):
        for t in range(mask_ref.shape[0]):
            value = mask_ref[t, b].astype(jnp.float32)
            seen_ref[b, :, t * tile : (t + 1) * tile] = jnp.full((1, tile), value, jnp.float32)
        return 0

    lax.fori_loop(0, B, fill, 0)
    down = lax.broadcasted_iota(jnp.int32, (NB, NB), 0)
    across = lax.broadcasted_iota(jnp.int32, (NB, NB), 1)
    for k in range(K):
        rows = slice(k * NB, (k + 1) * NB)
        again = slice(EE + k * NB, EE + (k + 1) * NB)
        m = jnp.where(down == across, 1.0, 0.0) - jnp.where(down == near_ref[k : k + 1], 1.0, 0.0)
        turned = m.T.astype(jnp.bfloat16)
        back_ref[:, rows] = m.astype(jnp.bfloat16)
        back_ref[:, again] = m.astype(jnp.bfloat16)
        diff_ref[rows, :NB] = turned
        diff_ref[rows, NB:] = turned
        weight_ref[rows] = jnp.broadcast_to(edge_ref[k : k + 1], (W, NB)).T

    gat[0] = user_ref[...]
    total[...] = jnp.zeros_like(total)
    lax.fori_loop(0, 2, functools.partial(gradient, True), 0)

    pl.semaphore_wait(barrier, NU - 1 + NI - 1)

    for q in range(NI - 1, 0, -1):
        for c in range(CHUNKS):
            gather(q, c).start()

    def give_dual(d):
        device = (along(d), i)
        return (
            send(snd_d.at[pl.ds(along(d) * T, T)], rec_d.at[u], d_s.at[d], d_r.at[d], device),
            send(snd_ds, rec_ds.at[u], ds_s.at[d], ds_r.at[d], device),
        )

    for d in range(1, NU):
        for copy in give_dual(d):
            copy.start()
    rec_d[u] = snd_d[pl.ds(u * T, T)]
    rec_ds[u] = dual_scale

    lax.fori_loop(2, STEPS, functools.partial(gradient, False), 0)

    def half(s):
        h = C >> (s + 1)
        base = 0
        for t in range(s):
            base = base + lax.rem(u // (1 << t), 2) * (C >> (t + 1))
        bit = lax.rem(u // (1 << s), 2)
        keep = pl.ds(pl.multiple_of(base + bit * h, h), h)
        away = pl.ds(pl.multiple_of(base + (1 - bit) * h, h), h)
        return keep, away, h

    def partner(s):
        return (flip(u, 1 << s, NU), i)

    def give_item(s):
        h = C >> (s + 1)
        return (
            send(snd_i.at[s, pl.ds(0, h)], rec_i.at[s, pl.ds(0, h)], i_s.at[s], i_r.at[s], partner(s)),
            send(snd_is.at[s], rec_is.at[s], is_s.at[s], is_r.at[s], partner(s)),
        )

    def halve_send(s):
        _, away, h = half(s)
        part = ired[away]
        inverse, scale = steps_of(peak(part))
        snd_i[s, pl.ds(0, h)] = coded(part, inverse)
        snd_is[s] = scale
        for copy in give_item(s):
            copy.start()

    def halve_take(s):
        keep, _, h = half(s)
        for copy in give_item(s):
            copy.wait_recv()
        ired[keep] += plain(rec_i[s, pl.ds(0, h)], rec_is[s])

    SEG = C // NU

    def give_all(s):
        keep, _, h = half(s)
        n = h // SEG
        base = 0
        for t in range(s + 1):
            base = base + lax.rem(u // (1 << t), 2) * ((C >> (t + 1)) // SEG)
        tile = pl.ds(base, n)
        return (
            send(gi.at[keep], gi.at[keep], a_s.at[s], a_r.at[s], partner(s)),
            send(gis.at[tile], gis.at[tile], as_s.at[s], as_r.at[s], partner(s)),
        )

    def double_first():
        keep, _, _ = half(LOG - 1)
        base = 0
        for t in range(LOG):
            base = base + lax.rem(u // (1 << t), 2) * (NU >> (t + 1))
        part = ired[keep]
        inverse, scale = steps_of(peak(part))
        gi[keep] = coded(part, inverse)
        gis[base] = scale

    def double_send(s):
        for copy in give_all(s):
            copy.start()

    def double_take(s):
        for copy in give_all(s):
            copy.wait_recv()

    ired[...] = total[...].T * item_scale
    halve_send(0)

    def close(c, m):
        g = own_part[c]
        for q in range(NI - 1, 0, -1):
            for copy in give_user(q, c):
                copy.wait_recv()
            g = g + plain(rec_u[q, c], rec_us[q, c])
        rows = pl.ds(pl.multiple_of(c * ROWS, ROWS), ROWS)
        t = user_ref[rows].astype(jnp.float32) - (descent * user_scale) * g
        tgt[rows] = t
        return jnp.maximum(m, peak(t))

    top = lax.fori_loop(0, CHUNKS, close, jnp.zeros((8, W), jnp.float32))
    target_inverse, target_scale = steps_of(jnp.max(top, axis=0, keepdims=True))
    snd_ts[...] = target_scale

    def turn_target(r, _):
        snd_t[r] = coded(tgt[pl.ds(r, B, stride=S), :], target_inverse)
        return 0

    lax.fori_loop(0, S, turn_target, 0, unroll=4)

    def give_target(d):
        device = (along(d), i)
        return (
            send(snd_t.at[pl.ds(along(d) * T, T)], rec_t.at[u], t_s.at[d], t_r.at[d], device),
            send(snd_ts, rec_ts.at[u], ts_s.at[d], ts_r.at[d], device),
        )

    for d in range(1, NU):
        for copy in give_target(d):
            copy.start()
    rec_t[u] = snd_t[pl.ds(u * T, T)]
    rec_ts[u] = target_scale

    halve_take(0)
    halve_send(1)

    for d in range(1, NU):
        for copy in give_dual(d):
            copy.wait_recv()
    for d in range(1, NU):
        for copy in give_target(d):
            copy.wait_recv()

    GROUP = 128

    def split(x):
        high = x.astype(jnp.bfloat16)
        return high, (x - high.astype(jnp.float32)).astype(jnp.bfloat16)

    def give_result(d, ch):
        device = (along(d), i)
        rows = pl.ds(ch * PAIR, PAIR)
        return (
            send(snd_r.at[along(d), rows], rec_r.at[u, rows], r_s.at[d, ch], r_r.at[d, ch], device),
            send(snd_rs.at[ch], rec_rs.at[u, ch], rs_s.at[d, ch], rs_r.at[d, ch], device),
        )

    def fold(m):
        m = jnp.max(m, axis=0, keepdims=True)
        out = m[:, :W]
        for n in range(1, PAIR):
            out = jnp.maximum(out, m[:, n * W : (n + 1) * W])
        return out

    def sweep_rows(ch, _):
        for n in range(PAIR):
            r = ch * PAIR + n
            lanes = slice(n * W, (n + 1) * W)
            for v in range(NU):
                xs[v * B : (v + 1) * B, lanes] = plain(rec_t[v, r], rec_ts[v])
                flux = plain(rec_d[v, r], rec_ds[v])
                for k in range(K):
                    fl[k * NB + v * B : k * NB + (v + 1) * B, lanes] = flux[k * B : (k + 1) * B]

        peaks = None
        for sweep in range(ITERS):
            source = xs[...] if sweep == 0 else ex[...]
            hl[:NB], hl[NB:] = split(source)
            peaks = jnp.zeros((8, PAIR * W), jnp.float32)
            for g in range(0, EE, GROUP):
                rows = slice(g, g + GROUP)
                slope = jnp.dot(diff_ref[rows], hl[...], preferred_element_type=jnp.float32)
                moved = fl[rows] + dual_step * slope
                w = weight_ref[rows]
                parts = []
                for n in range(PAIR):
                    m = moved[:, n * W : (n + 1) * W]
                    square = jnp.sum(m * m, axis=-1, keepdims=True)
                    parts.append(m * (w * lax.rsqrt(jnp.maximum(square, w * w))))
                flux = jnp.concatenate(parts, axis=1) if PAIR > 1 else parts[0]
                fl[rows] = flux
                fhl[rows], fhl[EE + g : EE + g + GROUP] = split(flux)
                peaks = jnp.maximum(peaks, peak(flux))
            div = jnp.dot(back_ref[...], fhl[...], preferred_element_type=jnp.float32)
            target = xs[...]
            if sweep == 0:
                primal = target
            newer = (primal - primal_step * div + primal_step * target) / (1.0 + primal_step)
            if sweep < ITERS - 1:
                ex[...] = 2.0 * newer - primal
            primal = newer

        flux_inverse, flux_scale = steps_of(fold(peaks))
        primal_inverse, primal_scale = steps_of(fold(peak(primal)))
        scales = jnp.concatenate([flux_scale, primal_scale], axis=0)
        snd_rs[ch] = scales
        for n in range(PAIR):
            r = ch * PAIR + n
            lanes = slice(n * W, (n + 1) * W)
            for v in range(NU):
                for k in range(K):
                    part = fl[k * NB + v * B : k * NB + (v + 1) * B, lanes]
                    snd_r[v, r, k * B : (k + 1) * B] = coded(part, flux_inverse)
                snd_r[v, r, E:] = coded(primal[v * B : (v + 1) * B, lanes], primal_inverse)
        for d in range(1, NU):
            for copy in give_result(d, ch):
                copy.start()
        rows = pl.ds(ch * PAIR, PAIR)
        rec_r[u, rows] = snd_r[u, rows]
        rec_rs[u, ch] = scales
        return 0

    PARTS = T // PAIR
    lax.fori_loop(0, PARTS, sweep_rows, 0)

    for s in range(1, LOG):
        halve_take(s)
        if s < LOG - 1:
            halve_send(s + 1)
    double_first()
    double_send(LOG - 1)

    def finish(ch, _):
        for d in range(1, NU):
            for copy in give_result(d, ch):
                copy.wait_recv()
        return 0

    for s in range(LOG - 1, 0, -1):
        double_take(s)
        double_send(s - 1)
    lax.fori_loop(0, PARTS, finish, 0)
    double_take(0)

    for q in range(1, NI):
        for c in range(CHUNKS):
            gather(q, c).wait_send()
            for copy in give_user(q, c):
                copy.wait_send()
    for d in range(1, NU):
        for copy in give_dual(d) + give_target(d):
            copy.wait_send()
        for ch in range(PARTS):
            for copy in give_result(d, ch):
                copy.wait_send()
    for s in range(LOG):
        for copy in give_item(s) + give_all(s):
            copy.wait_send()


def decode(dims, rec_r, rec_rs, gi, gis, out_p, out_d, out_i):
    NU, NI, B, S, K, C, W = dims
    T = S // NU
    PARTS = rec_rs.shape[1]
    PAIR = T // PARTS
    SEG = C // NU
    k = pl.program_id(0)
    flat_d = out_d.reshape(B * S, W)

    def place(v, _):
        for ch in range(PARTS):
            scales = rec_rs[v, ch]
            for t in range(ch * PAIR, (ch + 1) * PAIR):
                part = rec_r[v, t, pl.ds(pl.multiple_of(k * B, B), B)]
                flat_d[pl.ds(v * T + t, B, stride=S), :] = plain(part, scales[0:1])
        return 0

    lax.fori_loop(0, NU, place, 0)

    @pl.when(k == 0)
    def _():
        flat_p = out_p.reshape(B * S, W)

        def place(v, _):
            for ch in range(PARTS):
                scales = rec_rs[v, ch]
                for t in range(ch * PAIR, (ch + 1) * PAIR):
                    part = rec_r[v, t, B * K :]
                    flat_p[pl.ds(v * T + t, B, stride=S), :] = plain(part, scales[1:2])
            return 0

        lax.fori_loop(0, NU, place, 0)

    for n in range(NU // K):
        rows = slice(n * SEG, (n + 1) * SEG)
        out_i[rows] = plain(gi[rows], gis[n])


def shards(ratings, tile_mask, user_factors, item_factors, neighbours, edge_weight, dual):
    B, S, W = user_factors.shape
    K = neighbours.shape[1]
    NU = lax.axis_size("user")
    NI = lax.axis_size("item")
    C = item_factors.shape[0]
    T = S // NU
    E = B * K
    NB = B * NU
    EE = E * NU
    LOG = NU.bit_length() - 1
    ROWS = B // CHUNKS * S
    PAIR = 2 if T % 2 == 0 else 1
    PARTS = T // PAIR
    dims = (NU, NI, B, S, K, C, W)

    f32, i16, bf16 = jnp.float32, jnp.int16, jnp.bfloat16
    V = pltpu.VMEM
    dma = pltpu.SemaphoreType.DMA
    vmem = pl.BlockSpec(memory_space=pltpu.VMEM)
    smem = pl.BlockSpec(memory_space=pltpu.SMEM)
    scratch = [
        V((B, 1, C), f32), V((EE, 2 * NB), bf16), V((NB, 2 * EE), bf16), V((EE, W), f32),
        V((SLOTS, B // CHUNKS, S, C), bf16), V((NI, B * S, W), bf16), V((CHUNKS, ROWS, W), f32),
        V((W, C), f32),
        V((NI, CHUNKS, ROWS, W), i16), V((NI, CHUNKS, 8, W), f32),
        V((NI, CHUNKS, ROWS, W), i16), V((NI, CHUNKS, 8, W), f32),
        V((S, E, W), i16), V((1, W), f32), V((NU, T, E, W), i16), V((NU, 1, W), f32),
        V((B * S, W), f32), V((S, B, W), i16), V((1, W), f32), V((NU, T, B, W), i16), V((NU, 1, W), f32),
        V((NB, PAIR * W), f32), V((NB, PAIR * W), f32), V((2 * NB, PAIR * W), bf16),
        V((EE, PAIR * W), f32), V((2 * EE, PAIR * W), bf16),
        V((NU, T, E + B, W), i16), V((PARTS, 2, W), f32),
        V((C, W), f32), V((LOG, C // 2, W), i16), V((LOG, 8, W), f32),
        V((LOG, C // 2, W), i16), V((LOG, 8, W), f32),
        dma((SLOTS,)),
        *[dma((NI, CHUNKS)) for _ in range(6)],
        *[dma((NU,)) for _ in range(8)],
        *[dma((NU, PARTS)) for _ in range(4)],
        *[dma((LOG,)) for _ in range(8)],
    ]
    held = pl.pallas_call(
        functools.partial(kernel, dims),
        out_shape=(
            jax.ShapeDtypeStruct((NU, T, E + B, W), i16),
            jax.ShapeDtypeStruct((NU, PARTS, 2, W), f32),
            jax.ShapeDtypeStruct((C, W), i16),
            jax.ShapeDtypeStruct((NU, 8, W), f32),
        ),
        in_specs=[pl.BlockSpec(memory_space=pl.ANY), smem] + [vmem] * 5,
        out_specs=[vmem] * 4,
        scratch_shapes=scratch,
        compiler_params=pltpu.CompilerParams(
            collective_id=0, has_side_effects=True, vmem_limit_bytes=50 << 20
        ),
        cost_estimate=pl.CostEstimate(
            flops=6 * B * S * NI * C * W, bytes_accessed=2 * B * S * NI * C, transcendentals=0
        ),
    )(
        ratings.reshape(B, NI, S, C), tile_mask.T, user_factors.reshape(B * S, W), item_factors,
        dual.reshape(B * K * S, W), neighbours.T, edge_weight.T,
    )
    return pl.pallas_call(
        functools.partial(decode, dims),
        out_shape=(
            jax.ShapeDtypeStruct((B, S, W), f32),
            jax.ShapeDtypeStruct((B, K, S, W), f32),
            jax.ShapeDtypeStruct((C, W), f32),
        ),
        grid=(K,),
        in_specs=[
            pl.BlockSpec((NU, T, E + B, W), lambda k: (0, 0, 0, 0)),
            pl.BlockSpec((NU, PARTS, 2, W), lambda k: (0, 0, 0, 0)),
            pl.BlockSpec((C // K, W), lambda k: (k, 0)),
            pl.BlockSpec((NU // K, 8, W), lambda k: (k, 0, 0)),
        ],
        out_specs=[
            pl.BlockSpec((B, S, W), lambda k: (0, 0, 0)),
            pl.BlockSpec((B, 1, S, W), lambda k: (0, k, 0, 0)),
            pl.BlockSpec((C // K, W), lambda k: (k, 0)),
        ],
        compiler_params=pltpu.CompilerParams(vmem_limit_bytes=24 << 20),
        cost_estimate=pl.CostEstimate(
            flops=4 * B * (K + 1) * S * W, bytes_accessed=6 * B * (K + 1) * S * W, transcendentals=0
        ),
    )(*held)


def solution(mesh):
    in_specs = (
        P("user", "item"),
        P("user", "item"),
        P("user", "item", None),
        P("item", None),
        P(),
        P(),
        P("user", None, "item", None),
    )
    out_specs = (P("user", "item", None), P("user", None, "item", None), P("item", None))
    return jax.shard_map(shards, mesh=mesh, in_specs=in_specs, out_specs=out_specs, check_vma=False)
```

```python
import functools
import math

import jax
import jax.numpy as jnp
from jax import lax
from jax.experimental import pallas as pl
from jax.experimental.pallas import tpu as pltpu
from jax.sharding import PartitionSpec as P

ITERS = 2
TOP = 32767.0
TINY = 1e-30
CHUNKS = 4
SLOTS = 3
MESH = pl.DeviceIdType.MESH

descent = 0.5
dual_step = 0.5
primal_step = 0.25


def flip(index, mask, size):
    out, bit = 0, 1
    while bit < size:
        out = out + bit * lax.rem(index // bit + mask // bit, 2)
        bit *= 2
    return out


def tiles(x):
    return x.reshape(x.shape[0] // 8, 8, x.shape[1])


def peak(x):
    return jnp.max(jnp.abs(tiles(x)), axis=0)


def coded(x, inverse):
    y = tiles(x) * inverse[None]
    return jnp.round(y).astype(jnp.int32).astype(jnp.int16).reshape(x.shape)


def plain(q, scale):
    y = q.astype(jnp.int32).astype(jnp.float32)
    return (tiles(y) * scale[None]).reshape(q.shape)


def steps_of(top):
    top = jnp.maximum(top, TINY)
    return TOP / top, top * (1.0 / TOP)


def kernel(
    dims, rating_ref, mask_in, user_in, item_in, dual_in, near_in, edge_in,
    rec_r, rec_rs, gi, gis,
    mask_ref, user_ref, item_ref, dual_ref, near_ref, edge_ref, load_m, seen_ref, diff_ref, back_ref, weight_ref, rat, gat, own_part, kept, total, snd_u, snd_us, rec_u, rec_us,
    snd_d, snd_ds, rec_d, rec_ds, tgt, snd_t, snd_ts, rec_t, rec_ts,
    xs, ex, hl, fl, fhl, snd_r, snd_rs,
    ired, snd_i, snd_is, rec_i, rec_is,
    rat_m, ag_s, ag_r, u_s, u_r, us_s, us_r, d_s, d_r, ds_s, ds_r, t_s, t_r, ts_s, ts_r,
    r_s, r_r, rs_s, rs_r, i_s, i_r, is_s, is_r, a_s, a_r, as_s, as_r,
):
    NU, NI, B, S, K, C, W = dims
    T = S // NU
    E = B * K
    NB = B * NU
    EE = E * NU
    LOG = NU.bit_length() - 1
    PART = B // CHUNKS
    ROWS = PART * S
    STEPS = NI * CHUNKS
    PAIR = 2 if T % 2 == 0 else 1
    user_scale = 1.0 / math.sqrt(C * NI)
    item_scale = 1.0 / math.sqrt(B * S * NI * NU)

    u = lax.axis_index("user")
    i = lax.axis_index("item")

    def send(src, dst, s, r, device):
        return pltpu.make_async_remote_copy(
            src_ref=src, dst_ref=dst, send_sem=s, recv_sem=r, device_id=device, device_id_type=MESH
        )

    def along(d):
        return lax.rem(u + d, NU)

    def behind(d):
        return lax.rem(u + NU - d, NU)

    barrier = pltpu.get_barrier_semaphore()
    for d in range(1, NU):
        pl.semaphore_signal(barrier, inc=1, device_id=(along(d), i), device_id_type=MESH)
    for q in range(1, NI):
        pl.semaphore_signal(barrier, inc=1, device_id=(u, flip(i, q, NI)), device_id_type=MESH)

    loads = [
        pltpu.make_async_copy(src, dst, load_m.at[n])
        for n, (src, dst) in enumerate((
            (dual_in, dual_ref), (user_in, user_ref), (item_in, item_ref),
            (mask_in, mask_ref), (near_in, near_ref), (edge_in, edge_ref),
        ))
    ]
    for load in loads:
        load.start()

    EARLY = CHUNKS // 2
    FAR = (NI - 2) * CHUNKS

    def place(s):
        m = s - CHUNKS - EARLY
        p = m // CHUNKS
        far = 2 * (p // 2 + 1) + 1 - lax.rem(p, 2)
        q = jnp.where(s < CHUNKS, 0, jnp.where((m < 0) | (m >= FAR), 1, far))
        c = jnp.where(m < 0, lax.rem(s, CHUNKS), lax.rem(m, CHUNKS))
        c = jnp.where(m >= FAR, m - FAR + EARLY, c)
        return c, q

    def fetch(s):
        c, q = place(s)
        slot = lax.rem(s, SLOTS)
        return pltpu.make_async_copy(
            rating_ref.at[pl.ds(c * PART, PART), flip(i, q, NI)], rat.at[slot], rat_m.at[slot]
        )

    for s in range(SLOTS - 1):
        fetch(jnp.int32(s)).start()

    def gather(q, c):
        rows = pl.ds(pl.multiple_of(c * ROWS, ROWS), ROWS)
        return send(
            user_ref.at[rows], gat.at[q, rows], ag_s.at[q, c], ag_r.at[q, c], (u, flip(i, q, NI))
        )

    def pass_on(q, c):
        rows = pl.ds(pl.multiple_of(c * ROWS, ROWS), ROWS)
        return send(
            gat.at[q, rows], gat.at[q + 1, rows], ag_s.at[q + 1, c], ag_r.at[q + 1, c],
            (u, flip(i, 1, NI)),
        )

    def give_user(q, c):
        to = q * (1 - lax.rem(q, 2)) + lax.rem(q, 2)
        device = (u, flip(i, to, NI))
        return (
            send(snd_u.at[q, c], rec_u.at[q, c], u_s.at[q, c], u_r.at[q, c], device),
            send(snd_us.at[q, c], rec_us.at[q, c], us_s.at[q, c], us_r.at[q, c], device),
        )

    def gradient(s, _):
        c, q = place(s)
        slot = lax.rem(s, SLOTS)

        @pl.when(s + SLOTS - 1 < STEPS)
        def _():
            fetch(s + SLOTS - 1).start()

        if NI > 2:
            m = s - CHUNKS
            ahead = 2 * (m // (2 * CHUNKS) + 1)
            which = lax.rem(m, 2 * CHUNKS)

            @pl.when((m >= 0) & (ahead < NI) & (which < CHUNKS))
            def _():
                gather(ahead, which).wait_recv()
                pass_on(ahead, which).start()

        fetch(s).wait()

        @pl.when(lax.rem(q, 2) == 1)
        def _():
            gather(q, c).wait_recv()

        users = gat[q, pl.ds(pl.multiple_of(c * ROWS, ROWS), ROWS)]
        items = item_ref[...]
        scores = lax.dot_general(
            users, items, (((1,), (1,)), ((), ())), preferred_element_type=jnp.float32
        )
        error = scores.reshape(PART, S, C) - rat[slot].astype(jnp.float32)
        error = (seen_ref[pl.ds(c * PART, PART)] * error).astype(jnp.bfloat16).reshape(ROWS, C)
        total[...] += jnp.dot(users.T, error, preferred_element_type=jnp.float32)
        own_part[c] = jnp.dot(error, items, preferred_element_type=jnp.float32)

        @pl.when(q > 0)
        def _():
            @pl.when(lax.rem(q, 2) == 0)
            def _():
                for copy in give_user(q + 1, c):
                    copy.wait_recv()
                own_part[c] += plain(rec_u[q + 1, c], rec_us[q + 1, c])

            term = own_part[c]
            inverse, scale = steps_of(peak(term))
            snd_u[q, c] = coded(term, inverse)
            snd_us[q, c] = scale
            for copy in give_user(q, c):
                copy.start()

        @pl.when(q == 0)
        def _():
            kept[c] = own_part[c]

        return 0

    loads[0].wait()
    top = lax.fori_loop(
        0, B * K * S // 64,
        lambda k, m: jnp.maximum(m, peak(dual_ref[pl.ds(pl.multiple_of(k * 64, 64), 64)])),
        jnp.zeros((8, W), jnp.float32),
        unroll=4,
    )
    dual_inverse, dual_scale = steps_of(jnp.max(top, axis=0, keepdims=True))
    snd_ds[...] = dual_scale

    def turn_dual(r, _):
        for k in range(K):
            part = dual_ref[pl.ds(k * S + r, B, stride=K * S), :]
            snd_d[r, k * B : (k + 1) * B] = coded(part, dual_inverse)
        return 0

    lax.fori_loop(0, S, turn_dual, 0, unroll=4)
    for load in loads[1:]:
        load.wait()

    pl.semaphore_wait(barrier, NU - 1 + NI - 1)

    for c in range(CHUNKS):
        for q in range(2, NI, 2):
            gather(q, c).start()
        gather(1, c).start()

    def give_dual(d):
        device = (along(d), i)
        return (
            send(snd_d.at[pl.ds(along(d) * T, T)], rec_d.at[u], d_s.at[d], d_r.at[d], device),
            send(snd_ds, rec_ds.at[u], ds_s.at[d], ds_r.at[d], device),
        )

    for d in range(1, NU):
        for copy in give_dual(d):
            copy.start()

    spread = lax.broadcasted_iota(jnp.int32, (mask_ref.shape[0], C), 1) // (C // mask_ref.shape[0])
    spread = jnp.where(spread == lax.broadcasted_iota(jnp.int32, spread.shape, 0), 1.0, 0.0)
    seen = lax.dot_general(
        mask_ref[...].astype(jnp.float32), spread, (((0,), (0,)), ((), ())),
        preferred_element_type=jnp.float32,
    )
    for b in range(B):
        seen_ref[b] = seen[b : b + 1]
    gat[0] = user_ref[...]
    total[...] = jnp.zeros_like(total)
    lax.fori_loop(0, STEPS, gradient, 0)

    rec_d[u] = snd_d[pl.ds(u * T, T)]
    rec_ds[u] = dual_scale

    def half(s):
        h = C >> (s + 1)
        base = 0
        for t in range(s):
            base = base + lax.rem(u // (1 << t), 2) * (C >> (t + 1))
        bit = lax.rem(u // (1 << s), 2)
        keep = pl.ds(pl.multiple_of(base + bit * h, h), h)
        away = pl.ds(pl.multiple_of(base + (1 - bit) * h, h), h)
        return keep, away, h

    def partner(s):
        return (flip(u, 1 << s, NU), i)

    def give_item(s):
        h = C >> (s + 1)
        return (
            send(snd_i.at[s, pl.ds(0, h)], rec_i.at[s, pl.ds(0, h)], i_s.at[s], i_r.at[s], partner(s)),
            send(snd_is.at[s], rec_is.at[s], is_s.at[s], is_r.at[s], partner(s)),
        )

    def halve_send(s):
        _, away, h = half(s)
        part = ired[away]
        inverse, scale = steps_of(peak(part))
        snd_i[s, pl.ds(0, h)] = coded(part, inverse)
        snd_is[s] = scale
        for copy in give_item(s):
            copy.start()

    def halve_take(s):
        keep, _, h = half(s)
        for copy in give_item(s):
            copy.wait_recv()
        ired[keep] += plain(rec_i[s, pl.ds(0, h)], rec_is[s])

    SEG = C // NU

    def give_all(s):
        keep, _, h = half(s)
        n = h // SEG
        base = 0
        for t in range(s + 1):
            base = base + lax.rem(u // (1 << t), 2) * ((C >> (t + 1)) // SEG)
        tile = pl.ds(base, n)
        return (
            send(gi.at[keep], gi.at[keep], a_s.at[s], a_r.at[s], partner(s)),
            send(gis.at[tile], gis.at[tile], as_s.at[s], as_r.at[s], partner(s)),
        )

    def double_first():
        keep, _, _ = half(LOG - 1)
        base = 0
        for t in range(LOG):
            base = base + lax.rem(u // (1 << t), 2) * (NU >> (t + 1))
        part = ired[keep]
        inverse, scale = steps_of(peak(part))
        gi[keep] = coded(part, inverse)
        gis[base] = scale

    def double_send(s):
        for copy in give_all(s):
            copy.start()

    def double_take(s):
        for copy in give_all(s):
            copy.wait_recv()

    ired[...] = total[...].T * item_scale
    halve_send(0)

    def close(c, m):
        g = kept[c]
        for q in [*range(2, NI, 2), 1]:
            for copy in give_user(q, c):
                copy.wait_recv()
            g = g + plain(rec_u[q, c], rec_us[q, c])
        rows = pl.ds(pl.multiple_of(c * ROWS, ROWS), ROWS)
        t = user_ref[rows].astype(jnp.float32) - (descent * user_scale) * g
        tgt[rows] = t
        return jnp.maximum(m, peak(t))

    top = lax.fori_loop(0, CHUNKS, close, jnp.zeros((8, W), jnp.float32))
    target_inverse, target_scale = steps_of(jnp.max(top, axis=0, keepdims=True))
    snd_ts[...] = target_scale

    def turn_target(r, _):
        snd_t[r] = coded(tgt[pl.ds(r, B, stride=S), :], target_inverse)
        return 0

    lax.fori_loop(0, S, turn_target, 0, unroll=4)

    def give_target(d):
        device = (along(d), i)
        return (
            send(snd_t.at[pl.ds(along(d) * T, T)], rec_t.at[u], t_s.at[d], t_r.at[d], device),
            send(snd_ts, rec_ts.at[u], ts_s.at[d], ts_r.at[d], device),
        )

    for d in range(1, NU):
        for copy in give_target(d):
            copy.start()
    rec_t[u] = snd_t[pl.ds(u * T, T)]
    rec_ts[u] = target_scale

    down = lax.broadcasted_iota(jnp.int32, (NB, NB), 0)
    across = lax.broadcasted_iota(jnp.int32, (NB, NB), 1)
    for k in range(K):
        rows = slice(k * NB, (k + 1) * NB)
        again = slice(EE + k * NB, EE + (k + 1) * NB)
        m = jnp.where(down == across, 1.0, 0.0) - jnp.where(down == near_ref[k : k + 1], 1.0, 0.0)
        turned = m.T.astype(jnp.bfloat16)
        back_ref[:, rows] = m.astype(jnp.bfloat16)
        back_ref[:, again] = m.astype(jnp.bfloat16)
        diff_ref[rows, :NB] = turned
        diff_ref[rows, NB:] = turned
        weight_ref[rows] = jnp.broadcast_to(edge_ref[k : k + 1], (W, NB)).T

    chain = iter(range(2 * LOG))

    def item_step():
        s = next(chain, None)
        if s is None:
            return
        if s < LOG:
            halve_take(s)
            if s < LOG - 1:
                halve_send(s + 1)
            else:
                double_first()
                double_send(LOG - 1)
        else:
            s = 2 * LOG - 1 - s
            double_take(s)
            if s > 0:
                double_send(s - 1)

    item_step()

    for d in range(1, NU):
        for copy in give_dual(d):
            copy.wait_recv()
    for d in range(1, NU):
        for copy in give_target(d):
            copy.wait_recv()

    GROUP = 128

    def split(x):
        high = x.astype(jnp.bfloat16)
        return high, (x - high.astype(jnp.float32)).astype(jnp.bfloat16)

    def give_result(d, ch):
        device = (along(d), i)
        rows = pl.ds(ch * PAIR, PAIR)
        return (
            send(snd_r.at[along(d), rows], rec_r.at[u, rows], r_s.at[d, ch], r_r.at[d, ch], device),
            send(snd_rs.at[ch], rec_rs.at[u, ch], rs_s.at[d, ch], rs_r.at[d, ch], device),
        )

    def fold(m):
        m = jnp.max(m, axis=0, keepdims=True)
        out = m[:, :W]
        for n in range(1, PAIR):
            out = jnp.maximum(out, m[:, n * W : (n + 1) * W])
        return out

    def sweep_rows(ch, _):
        for n in range(PAIR):
            r = ch * PAIR + n
            lanes = slice(n * W, (n + 1) * W)
            for v in range(NU):
                xs[v * B : (v + 1) * B, lanes] = plain(rec_t[v, r], rec_ts[v])
                flux = plain(rec_d[v, r], rec_ds[v])
                for k in range(K):
                    fl[k * NB + v * B : k * NB + (v + 1) * B, lanes] = flux[k * B : (k + 1) * B]

        peaks = None
        for sweep in range(ITERS):
            source = xs[...] if sweep == 0 else ex[...]
            hl[:NB], hl[NB:] = split(source)
            peaks = jnp.zeros((8, PAIR * W), jnp.float32)
            for g in range(0, EE, GROUP):
                rows = slice(g, g + GROUP)
                slope = jnp.dot(diff_ref[rows], hl[...], preferred_element_type=jnp.float32)
                moved = fl[rows] + dual_step * slope
                w = weight_ref[rows]
                parts = []
                for n in range(PAIR):
                    m = moved[:, n * W : (n + 1) * W]
                    square = jnp.sum(m * m, axis=-1, keepdims=True)
                    parts.append(m * (w * lax.rsqrt(jnp.maximum(square, w * w))))
                flux = jnp.concatenate(parts, axis=1) if PAIR > 1 else parts[0]
                fl[rows] = flux
                fhl[rows], fhl[EE + g : EE + g + GROUP] = split(flux)
                peaks = jnp.maximum(peaks, peak(flux))
            div = jnp.dot(back_ref[...], fhl[...], preferred_element_type=jnp.float32)
            target = xs[...]
            if sweep == 0:
                primal = target
            newer = (primal - primal_step * div + primal_step * target) / (1.0 + primal_step)
            if sweep < ITERS - 1:
                ex[...] = 2.0 * newer - primal
            primal = newer

        flux_inverse, flux_scale = steps_of(fold(peaks))
        primal_inverse, primal_scale = steps_of(fold(peak(primal)))
        scales = jnp.concatenate([flux_scale, primal_scale], axis=0)
        snd_rs[ch] = scales
        for n in range(PAIR):
            r = ch * PAIR + n
            lanes = slice(n * W, (n + 1) * W)
            for v in range(NU):
                for k in range(K):
                    part = fl[k * NB + v * B : k * NB + (v + 1) * B, lanes]
                    snd_r[v, r, k * B : (k + 1) * B] = coded(part, flux_inverse)
                snd_r[v, r, E:] = coded(primal[v * B : (v + 1) * B, lanes], primal_inverse)
        rows = pl.ds(ch * PAIR, PAIR)
        rec_r[u, rows] = snd_r[u, rows]
        rec_rs[u, ch] = scales

        if PARTS > 1:
            @pl.when(ch == 1)
            def _():
                item_step()

        @pl.when(ch < 2)
        def _():
            for d in range(1, NU):
                for copy in give_result(d, ch):
                    copy.start()

        return 0

    PARTS = T // PAIR
    lax.fori_loop(0, PARTS, sweep_rows, 0)

    for ch in range(PARTS):
        for d in range(1, NU):
            for copy in give_result(d, ch):
                copy.wait_recv()
        item_step()
        if ch + 2 < PARTS:
            for d in range(1, NU):
                for copy in give_result(d, ch + 2):
                    copy.start()
    for _ in range(2 * LOG):
        item_step()

    for q in range(1, NI):
        for c in range(CHUNKS):
            (pass_on(q - 1, c) if q > 1 and q % 2 else gather(q, c)).wait_send()
            for copy in give_user(q, c):
                copy.wait_send()
    for d in range(1, NU):
        for copy in give_dual(d) + give_target(d):
            copy.wait_send()
        for ch in range(PARTS):
            for copy in give_result(d, ch):
                copy.wait_send()
    for s in range(LOG):
        for copy in give_item(s) + give_all(s):
            copy.wait_send()


def decode(dims, rec_r, rec_rs, gi, gis, out_p, out_d, out_i):
    NU, NI, B, S, K, C, W = dims
    T = S // NU
    PARTS = rec_rs.shape[1]
    PAIR = T // PARTS
    SEG = C // NU
    k = pl.program_id(0)
    flat_d = out_d.reshape(B * S, W)

    def place(v, _):
        for ch in range(PARTS):
            scales = rec_rs[v, ch]
            for t in range(ch * PAIR, (ch + 1) * PAIR):
                part = rec_r[v, t, pl.ds(pl.multiple_of(k * B, B), B)]
                flat_d[pl.ds(v * T + t, B, stride=S), :] = plain(part, scales[0:1])
        return 0

    lax.fori_loop(0, NU, place, 0)

    @pl.when(k == 0)
    def _():
        flat_p = out_p.reshape(B * S, W)

        def place(v, _):
            for ch in range(PARTS):
                scales = rec_rs[v, ch]
                for t in range(ch * PAIR, (ch + 1) * PAIR):
                    part = rec_r[v, t, B * K :]
                    flat_p[pl.ds(v * T + t, B, stride=S), :] = plain(part, scales[1:2])
            return 0

        lax.fori_loop(0, NU, place, 0)

    for n in range(NU // K):
        rows = slice(n * SEG, (n + 1) * SEG)
        out_i[rows] = plain(gi[rows], gis[n])


def shards(ratings, tile_mask, user_factors, item_factors, neighbours, edge_weight, dual):
    B, S, W = user_factors.shape
    K = neighbours.shape[1]
    NU = lax.axis_size("user")
    NI = lax.axis_size("item")
    C = item_factors.shape[0]
    T = S // NU
    E = B * K
    NB = B * NU
    EE = E * NU
    LOG = NU.bit_length() - 1
    ROWS = B // CHUNKS * S
    PAIR = 2 if T % 2 == 0 else 1
    PARTS = T // PAIR
    dims = (NU, NI, B, S, K, C, W)

    f32, i16, bf16 = jnp.float32, jnp.int16, jnp.bfloat16
    V = pltpu.VMEM
    dma = pltpu.SemaphoreType.DMA
    vmem = pl.BlockSpec(memory_space=pltpu.VMEM)
    hbm = pl.BlockSpec(memory_space=pltpu.HBM)
    scratch = [
        V((tile_mask.shape[1], B), jnp.int32), V((B * S, W), bf16), V((C, W), bf16), V((B * K * S, W), f32),
        V((K, NB), jnp.int32), V((K, NB), f32), dma((6,)), V((B, 1, C), f32), V((EE, 2 * NB), bf16), V((NB, 2 * EE), bf16), V((EE, W), f32),
        V((SLOTS, B // CHUNKS, S, C), bf16), V((NI, B * S, W), bf16), V((CHUNKS, ROWS, W), f32),
        V((CHUNKS, ROWS, W), f32), V((W, C), f32),
        V((NI, CHUNKS, ROWS, W), i16), V((NI, CHUNKS, 8, W), f32),
        V((NI, CHUNKS, ROWS, W), i16), V((NI, CHUNKS, 8, W), f32),
        V((S, E, W), i16), V((1, W), f32), V((NU, T, E, W), i16), V((NU, 1, W), f32),
        V((B * S, W), f32), V((S, B, W), i16), V((1, W), f32), V((NU, T, B, W), i16), V((NU, 1, W), f32),
        V((NB, PAIR * W), f32), V((NB, PAIR * W), f32), V((2 * NB, PAIR * W), bf16),
        V((EE, PAIR * W), f32), V((2 * EE, PAIR * W), bf16),
        V((NU, T, E + B, W), i16), V((PARTS, 2, W), f32),
        V((C, W), f32), V((LOG, C // 2, W), i16), V((LOG, 8, W), f32),
        V((LOG, C // 2, W), i16), V((LOG, 8, W), f32),
        dma((SLOTS,)),
        *[dma((NI, CHUNKS)) for _ in range(6)],
        *[dma((NU,)) for _ in range(8)],
        *[dma((NU, PARTS)) for _ in range(4)],
        *[dma((LOG,)) for _ in range(8)],
    ]
    held = pl.pallas_call(
        functools.partial(kernel, dims),
        out_shape=(
            jax.ShapeDtypeStruct((NU, T, E + B, W), i16),
            jax.ShapeDtypeStruct((NU, PARTS, 2, W), f32),
            jax.ShapeDtypeStruct((C, W), i16),
            jax.ShapeDtypeStruct((NU, 8, W), f32),
        ),
        in_specs=[hbm] * 7,
        out_specs=[vmem] * 4,
        scratch_shapes=scratch,
        compiler_params=pltpu.CompilerParams(
            collective_id=0, has_side_effects=True, vmem_limit_bytes=61 << 20
        ),
        cost_estimate=pl.CostEstimate(
            flops=6 * B * S * NI * C * W, bytes_accessed=2 * B * S * NI * C, transcendentals=0
        ),
    )(
        ratings.reshape(B, NI, S, C), tile_mask.T, user_factors.reshape(B * S, W), item_factors,
        dual.reshape(B * K * S, W), neighbours.T, edge_weight.T,
    )
    return pl.pallas_call(
        functools.partial(decode, dims),
        out_shape=(
            jax.ShapeDtypeStruct((B, S, W), f32),
            jax.ShapeDtypeStruct((B, K, S, W), f32),
            jax.ShapeDtypeStruct((C, W), f32),
        ),
        grid=(K,),
        in_specs=[
            pl.BlockSpec((NU, T, E + B, W), lambda k: (0, 0, 0, 0)),
            pl.BlockSpec((NU, PARTS, 2, W), lambda k: (0, 0, 0, 0)),
            pl.BlockSpec((C // K, W), lambda k: (k, 0)),
            pl.BlockSpec((NU // K, 8, W), lambda k: (k, 0, 0)),
        ],
        out_specs=[
            pl.BlockSpec((B, S, W), lambda k: (0, 0, 0)),
            pl.BlockSpec((B, 1, S, W), lambda k: (0, k, 0, 0)),
            pl.BlockSpec((C // K, W), lambda k: (k, 0)),
        ],
        compiler_params=pltpu.CompilerParams(vmem_limit_bytes=61 << 20),
        cost_estimate=pl.CostEstimate(
            flops=4 * B * (K + 1) * S * W, bytes_accessed=6 * B * (K + 1) * S * W, transcendentals=0
        ),
    )(*held)


def solution(mesh):
    in_specs = (
        P("user", "item"),
        P("user", "item"),
        P("user", "item", None),
        P("item", None),
        P(),
        P(),
        P("user", None, "item", None),
    )
    out_specs = (P("user", "item", None), P("user", None, "item", None), P("item", None))
    return jax.shard_map(shards, mesh=mesh, in_specs=in_specs, out_specs=out_specs, check_vma=False)
```

```python
import functools
import math

import jax
import jax.numpy as jnp
from jax import lax
from jax.experimental import pallas as pl
from jax.experimental.pallas import tpu as pltpu
from jax.sharding import PartitionSpec as P

ITERS = 2
TOP = 32767.0
TINY = 1e-30
CHUNKS = 2
LEAD = 3
SLOTS = 3
MESH = pl.DeviceIdType.MESH

descent = 0.5
dual_step = 0.5
primal_step = 0.25


def flip(index, mask, size):
    out, bit = 0, 1
    while bit < size:
        out = out + bit * lax.rem(index // bit + mask // bit, 2)
        bit *= 2
    return out


def tiles(x):
    return x.reshape(x.shape[0] // 8, 8, x.shape[1])


def peak(x):
    return jnp.max(jnp.abs(tiles(x)), axis=0)


def coded(x, inverse):
    y = tiles(x) * inverse[None]
    return jnp.round(y).astype(jnp.int32).astype(jnp.int16).reshape(x.shape)


def turned(x, inverse):
    y = jnp.swapaxes(x, 0, 1) * inverse[None]
    return jnp.round(y).astype(jnp.int32).astype(jnp.int16)


def plain(q, scale):
    y = q.astype(jnp.int32).astype(jnp.float32)
    return (tiles(y) * scale[None]).reshape(q.shape)


def steps_of(top):
    top = jnp.maximum(top, TINY)
    return TOP / top, top * (1.0 / TOP)


def kernel(
    dims, rating_ref, mask_in, user_in, item_in, dual_in, near_in, edge_in,
    rec_r, rec_rs, gi, gis,
    mask_ref, user_ref, item_ref, dual_ref, near_ref, edge_ref, load_m, seen_ref, diff_ref, back_ref, weight_ref, rat, gat, own_part, kept, total, snd_u, snd_us, rec_u, rec_us,
    snd_d, snd_ds, rec_d, rec_ds, tgt, snd_t, snd_ts, rec_t, rec_ts,
    xs, ex, hl, fl, fhl, snd_r, snd_rs,
    ired, snd_i, snd_is, rec_i, rec_is,
    rat_m, ag_s, ag_r, u_s, u_r, us_s, us_r, d_s, d_r, ds_s, ds_r, t_s, t_r, ts_s, ts_r,
    r_s, r_r, rs_s, rs_r, i_s, i_r, is_s, is_r, a_s, a_r, as_s, as_r,
):
    NU, NI, B, S, K, C, W = dims
    T = S // NU
    E = B * K
    NB = B * NU
    EE = E * NU
    LOG = NU.bit_length() - 1
    PART = B // CHUNKS
    ROWS = PART * S
    STEPS = NI * CHUNKS
    PAIR = 2 if T % 2 == 0 else 1
    PARTS = T // PAIR
    user_scale = 1.0 / math.sqrt(C * NI)
    item_scale = 1.0 / math.sqrt(B * S * NI * NU)

    u = lax.axis_index("user")
    i = lax.axis_index("item")

    def send(src, dst, s, r, device):
        return pltpu.make_async_remote_copy(
            src_ref=src, dst_ref=dst, send_sem=s, recv_sem=r, device_id=device, device_id_type=MESH
        )

    def along(d):
        return lax.rem(u + d, NU)

    def behind(d):
        return lax.rem(u + NU - d, NU)

    barrier = pltpu.get_barrier_semaphore()
    for d in range(1, NU):
        pl.semaphore_signal(barrier, inc=1, device_id=(along(d), i), device_id_type=MESH)
    for q in range(1, NI):
        pl.semaphore_signal(barrier, inc=1, device_id=(u, flip(i, q, NI)), device_id_type=MESH)

    loads = [
        pltpu.make_async_copy(src, dst, load_m.at[n])
        for n, (src, dst) in enumerate((
            (dual_in, dual_ref), (user_in, user_ref), (item_in, item_ref),
            (mask_in, mask_ref), (near_in, near_ref), (edge_in, edge_ref),
        ))
    ]
    for load in loads:
        load.start()

    EARLY = CHUNKS // 2
    FAR = (NI - 2) * CHUNKS

    def place(s):
        m = s - CHUNKS - EARLY
        p = m // CHUNKS
        far = 2 * (p // 2 + 1) + 1 - lax.rem(p, 2)
        q = jnp.where(s < CHUNKS, 0, jnp.where((m < 0) | (m >= FAR), 1, far))
        c = jnp.where(m < 0, lax.rem(s, CHUNKS), lax.rem(m, CHUNKS))
        c = jnp.where(m >= FAR, m - FAR + EARLY, c)
        return c, q

    def fetch(s):
        c, q = place(s)
        slot = lax.rem(s, SLOTS)
        return pltpu.make_async_copy(
            rating_ref.at[pl.ds(c * PART, PART), flip(i, q, NI)], rat.at[slot], rat_m.at[slot]
        )

    for s in range(SLOTS - 1):
        fetch(jnp.int32(s)).start()

    def gather(q, c):
        rows = pl.ds(pl.multiple_of(c * ROWS, ROWS), ROWS)
        return send(
            user_ref.at[rows], gat.at[q, rows], ag_s.at[q, c], ag_r.at[q, c], (u, flip(i, q, NI))
        )

    def pass_on(q, c):
        rows = pl.ds(pl.multiple_of(c * ROWS, ROWS), ROWS)
        return send(
            gat.at[q, rows], gat.at[q + 1, rows], ag_s.at[q + 1, c], ag_r.at[q + 1, c],
            (u, flip(i, 1, NI)),
        )

    def give_user(q, c):
        to = q * (1 - lax.rem(q, 2)) + lax.rem(q, 2)
        device = (u, flip(i, to, NI))
        return (
            send(snd_u.at[q, c], rec_u.at[q, c], u_s.at[q, c], u_r.at[q, c], device),
            send(snd_us.at[q, c], rec_us.at[q, c], us_s.at[q, c], us_r.at[q, c], device),
        )

    def gradient(s, _):
        c, q = place(s)
        slot = lax.rem(s, SLOTS)

        @pl.when(s + SLOTS - 1 < STEPS)
        def _():
            fetch(s + SLOTS - 1).start()

        if NI > 2:
            m = s - CHUNKS
            ahead = 2 * (m // (2 * CHUNKS) + 1)
            which = lax.rem(m, 2 * CHUNKS)

            @pl.when((m >= 0) & (ahead < NI) & (which < CHUNKS))
            def _():
                gather(ahead, which).wait_recv()
                pass_on(ahead, which).start()

        fetch(s).wait()

        @pl.when(lax.rem(q, 2) == 1)
        def _():
            gather(q, c).wait_recv()

        users = gat[q, pl.ds(pl.multiple_of(c * ROWS, ROWS), ROWS)]
        items = item_ref[...]
        scores = lax.dot_general(
            users, items, (((1,), (1,)), ((), ())), preferred_element_type=jnp.float32
        )
        error = scores.reshape(PART, S, C) - rat[slot].astype(jnp.float32)
        error = (seen_ref[pl.ds(c * PART, PART)] * error).astype(jnp.bfloat16).reshape(ROWS, C)
        total[...] += jnp.dot(users.T, error, preferred_element_type=jnp.float32)
        own_part[c] = jnp.dot(error, items, preferred_element_type=jnp.float32)

        @pl.when(q > 0)
        def _():
            @pl.when(lax.rem(q, 2) == 0)
            def _():
                for copy in give_user(q + 1, c):
                    copy.wait_recv()
                own_part[c] += plain(rec_u[q + 1, c], rec_us[q + 1, c])

            term = own_part[c]
            inverse, scale = steps_of(peak(term))
            snd_u[q, c] = coded(term, inverse)
            snd_us[q, c] = scale
            for copy in give_user(q, c):
                copy.start()

        @pl.when(q == 0)
        def _():
            kept[c] = own_part[c]

        return 0

    loads[0].wait()
    top = lax.fori_loop(
        0, B,
        lambda b, m: jnp.maximum(m, peak(dual_ref[b].reshape(K * S, W))),
        jnp.zeros((8, W), jnp.float32),
    )
    dual_inverse, dual_scale = steps_of(jnp.max(top, axis=0, keepdims=True))
    snd_ds[...] = dual_scale

    def turn_dual(g, _):
        rows = pl.ds(pl.multiple_of(g * 8, 8), 8)
        for k in range(K):
            snd_d[rows, k * B : (k + 1) * B] = turned(dual_ref[:, k, rows, :], dual_inverse)
        return 0

    lax.fori_loop(0, S // 8, turn_dual, 0)
    for load in loads[1:]:
        load.wait()

    pl.semaphore_wait(barrier, NU - 1 + NI - 1)

    for c in range(CHUNKS):
        for q in range(2, NI, 2):
            gather(q, c).start()
        gather(1, c).start()

    def give_dual(d):
        device = (along(d), i)
        return (
            send(snd_d.at[pl.ds(along(d) * T, T)], rec_d.at[u], d_s.at[d], d_r.at[d], device),
            send(snd_ds, rec_ds.at[u], ds_s.at[d], ds_r.at[d], device),
        )

    for d in range(1, NU):
        for copy in give_dual(d):
            copy.start()

    spread = lax.broadcasted_iota(jnp.int32, (mask_ref.shape[0], C), 1) // (C // mask_ref.shape[0])
    spread = jnp.where(spread == lax.broadcasted_iota(jnp.int32, spread.shape, 0), 1.0, 0.0)
    seen = lax.dot_general(
        mask_ref[...].astype(jnp.float32), spread, (((0,), (0,)), ((), ())),
        preferred_element_type=jnp.float32,
    )
    for b in range(B):
        seen_ref[b] = seen[b : b + 1]
    gat[0] = user_ref[...]
    total[...] = jnp.zeros_like(total)
    lax.fori_loop(0, STEPS, gradient, 0)

    rec_d[u] = snd_d[pl.ds(u * T, T)]
    rec_ds[u] = dual_scale

    def half(s):
        h = C >> (s + 1)
        base = 0
        for t in range(s):
            base = base + lax.rem(u // (1 << t), 2) * (C >> (t + 1))
        bit = lax.rem(u // (1 << s), 2)
        keep = pl.ds(pl.multiple_of(base + bit * h, h), h)
        away = pl.ds(pl.multiple_of(base + (1 - bit) * h, h), h)
        return keep, away, h

    def partner(s):
        return (flip(u, 1 << s, NU), i)

    LAST = LOG - 1

    def give_item(s):
        h = C >> min(s + 1, LAST)
        return (
            send(snd_i.at[s, pl.ds(0, h)], rec_i.at[s, pl.ds(0, h)], i_s.at[s], i_r.at[s], partner(s)),
            send(snd_is.at[s], rec_is.at[s], is_s.at[s], is_r.at[s], partner(s)),
        )

    def halve_send(s):
        if s < LAST:
            _, away, h = half(s)
        else:
            away, _, h = half(LAST - 1)
        part = ired[away]
        inverse, scale = steps_of(peak(part))
        snd_i[s, pl.ds(0, h)] = coded(part, inverse)
        snd_is[s] = scale
        if s == LAST:
            ired[away] = plain(snd_i[s, pl.ds(0, h)], scale)
        for copy in give_item(s):
            copy.start()

    def halve_take(s):
        keep, _, h = half(min(s, LAST - 1))
        for copy in give_item(s):
            copy.wait_recv()
        ired[keep] += plain(rec_i[s, pl.ds(0, h)], rec_is[s])

    SEG = C >> LAST

    def give_all(s):
        keep, _, h = half(s)
        n = h // SEG
        base = 0
        for t in range(s + 1):
            base = base + lax.rem(u // (1 << t), 2) * ((C >> (t + 1)) // SEG)
        tile = pl.ds(base, n)
        return (
            send(gi.at[keep], gi.at[keep], a_s.at[s], a_r.at[s], partner(s)),
            send(gis.at[tile], gis.at[tile], as_s.at[s], as_r.at[s], partner(s)),
        )

    def double_first():
        keep, _, _ = half(LAST - 1)
        base = 0
        for t in range(LAST):
            base = base + lax.rem(u // (1 << t), 2) * (NU >> (t + 2))
        part = ired[keep]
        inverse, scale = steps_of(peak(part))
        gi[keep] = coded(part, inverse)
        gis[base] = scale

    def double_send(s):
        for copy in give_all(s):
            copy.start()

    def double_take(s):
        for copy in give_all(s):
            copy.wait_recv()

    def close(c, m):
        g = kept[c]
        for q in [*range(2, NI, 2), 1]:
            for copy in give_user(q, c):
                copy.wait_recv()
            g = g + plain(rec_u[q, c], rec_us[q, c])
        rows = pl.ds(pl.multiple_of(c * ROWS, ROWS), ROWS)
        t = user_ref[rows].astype(jnp.float32) - (descent * user_scale) * g
        tgt[pl.ds(c * PART, PART)] = t.reshape(PART, S, W)
        return jnp.maximum(m, peak(t))

    top = lax.fori_loop(0, CHUNKS, close, jnp.zeros((8, W), jnp.float32))
    target_inverse, target_scale = steps_of(jnp.max(top, axis=0, keepdims=True))
    snd_ts[...] = target_scale

    def turn_target(g, _):
        rows = pl.ds(pl.multiple_of(g * 8, 8), 8)
        snd_t[rows] = turned(tgt[:, rows, :], target_inverse)
        return 0

    lax.fori_loop(0, S // 8, turn_target, 0)

    def give_scale(d):
        return send(snd_ts, rec_ts.at[u], ts_s.at[d], ts_r.at[d], (along(d), i))

    def give_target(d, ch):
        return send(
            snd_t.at[pl.ds(along(d) * T + ch * PAIR, PAIR)], rec_t.at[u, pl.ds(ch * PAIR, PAIR)],
            t_s.at[d, ch], t_r.at[d, ch], (along(d), i),
        )

    for d in range(1, NU):
        give_scale(d).start()
    for ch in range(PARTS):
        for d in range(1, NU):
            give_target(d, ch).start()
    ired[...] = total[...].T * item_scale
    halve_send(0)
    rec_t[u] = snd_t[pl.ds(u * T, T)]
    rec_ts[u] = target_scale

    down = lax.broadcasted_iota(jnp.int32, (NB, NB), 0)
    across = lax.broadcasted_iota(jnp.int32, (NB, NB), 1)
    for k in range(K):
        rows = slice(k * NB, (k + 1) * NB)
        again = slice(EE + k * NB, EE + (k + 1) * NB)
        m = jnp.where(down == across, 1.0, 0.0) - jnp.where(down == near_ref[k : k + 1], 1.0, 0.0)
        side = m.T.astype(jnp.bfloat16)
        back_ref[:, rows] = m.astype(jnp.bfloat16)
        back_ref[:, again] = m.astype(jnp.bfloat16)
        diff_ref[rows, :NB] = side
        diff_ref[rows, NB:] = side
        weight_ref[rows] = jnp.broadcast_to(edge_ref[k : k + 1], (W, NB)).T

    chain = iter(range(LOG + LAST))

    def item_step():
        s = next(chain, None)
        if s is None:
            return
        if s < LOG:
            halve_take(s)
            if s < LAST:
                halve_send(s + 1)
            else:
                double_first()
                double_send(LAST - 1)
        else:
            s = LOG + LAST - 1 - s
            double_take(s)
            if s > 0:
                double_send(s - 1)

    for d in range(1, NU):
        for copy in give_dual(d):
            copy.wait_recv()
    for d in range(1, NU):
        give_scale(d).wait_recv()

    GROUP = 128

    def split(x):
        high = x.astype(jnp.bfloat16)
        return high, (x - high.astype(jnp.float32)).astype(jnp.bfloat16)

    def give_result(d, ch):
        device = (along(d), i)
        rows = pl.ds(ch * PAIR, PAIR)
        return (
            send(snd_r.at[along(d), rows], rec_r.at[u, rows], r_s.at[d, ch], r_r.at[d, ch], device),
            send(snd_rs.at[ch], rec_rs.at[u, ch], rs_s.at[d, ch], rs_r.at[d, ch], device),
        )

    def fold(m):
        m = jnp.max(m, axis=0, keepdims=True)
        out = m[:, :W]
        for n in range(1, PAIR):
            out = jnp.maximum(out, m[:, n * W : (n + 1) * W])
        return out

    CUT = NU // 2

    def unit(n):
        return n // 2, range(1, CUT) if n % 2 == 0 else range(CUT, NU)

    def unit_start(n):
        ch, ds = unit(n)
        for d in ds:
            for copy in give_result(d, ch):
                copy.start()

    def unit_wait(n):
        ch, ds = unit(n)
        for d in ds:
            for copy in give_result(d, ch):
                copy.wait_recv()

    def sweep_rows(ch, _):
        for d in range(1, NU):
            give_target(d, ch).wait_recv()
        for n in range(PAIR):
            r = ch * PAIR + n
            lanes = slice(n * W, (n + 1) * W)
            for v in range(NU):
                xs[v * B : (v + 1) * B, lanes] = plain(rec_t[v, r], rec_ts[v])
                flux = plain(rec_d[v, r], rec_ds[v])
                for k in range(K):
                    fl[k * NB + v * B : k * NB + (v + 1) * B, lanes] = flux[k * B : (k + 1) * B]

        peaks = None
        for sweep in range(ITERS):
            source = xs[...] if sweep == 0 else ex[...]
            hl[:NB], hl[NB:] = split(source)
            peaks = jnp.zeros((8, PAIR * W), jnp.float32)
            for g in range(0, EE, GROUP):
                rows = slice(g, g + GROUP)
                slope = jnp.dot(diff_ref[rows], hl[...], preferred_element_type=jnp.float32)
                moved = fl[rows] + dual_step * slope
                w = weight_ref[rows]
                parts = []
                for n in range(PAIR):
                    m = moved[:, n * W : (n + 1) * W]
                    square = jnp.sum(m * m, axis=-1, keepdims=True)
                    parts.append(m * (w * lax.rsqrt(jnp.maximum(square, w * w))))
                flux = jnp.concatenate(parts, axis=1) if PAIR > 1 else parts[0]
                fl[rows] = flux
                fhl[rows], fhl[EE + g : EE + g + GROUP] = split(flux)
                peaks = jnp.maximum(peaks, peak(flux))
            div = jnp.dot(back_ref[...], fhl[...], preferred_element_type=jnp.float32)
            target = xs[...]
            if sweep == 0:
                primal = target
            newer = (primal - primal_step * div + primal_step * target) / (1.0 + primal_step)
            if sweep < ITERS - 1:
                ex[...] = 2.0 * newer - primal
            primal = newer

        flux_inverse, flux_scale = steps_of(fold(peaks))
        primal_inverse, primal_scale = steps_of(fold(peak(primal)))
        scales = jnp.concatenate([flux_scale, primal_scale], axis=0)
        snd_rs[ch] = scales
        for n in range(PAIR):
            r = ch * PAIR + n
            lanes = slice(n * W, (n + 1) * W)
            for v in range(NU):
                for k in range(K):
                    part = fl[k * NB + v * B : k * NB + (v + 1) * B, lanes]
                    snd_r[v, r, k * B : (k + 1) * B] = coded(part, flux_inverse)
                snd_r[v, r, E:] = coded(primal[v * B : (v + 1) * B, lanes], primal_inverse)
        rows = pl.ds(ch * PAIR, PAIR)
        rec_r[u, rows] = snd_r[u, rows]
        rec_rs[u, ch] = scales

        for n in range(min(LEAD, 2 * PARTS)):
            @pl.when(ch == n // 2)
            def _():
                if n == 2:
                    item_step()
                unit_start(n)

        return 0

    lax.fori_loop(0, PARTS, sweep_rows, 0)

    for n in range(2 * PARTS):
        unit_wait(n)
        if n % 2 == 0:
            item_step()
        if n + LEAD < 2 * PARTS:
            unit_start(n + LEAD)
    for _ in range(2 * LOG):
        item_step()

    for q in range(1, NI):
        for c in range(CHUNKS):
            (pass_on(q - 1, c) if q > 1 and q % 2 else gather(q, c)).wait_send()
            for copy in give_user(q, c):
                copy.wait_send()
    for d in range(1, NU):
        for copy in give_dual(d) + (give_scale(d),):
            copy.wait_send()
        for ch in range(PARTS):
            give_target(d, ch).wait_send()
            for copy in give_result(d, ch):
                copy.wait_send()
    for s in range(LOG):
        for copy in give_item(s) + (give_all(s) if s < LAST else ()):
            copy.wait_send()


def decode(dims, rec_r, rec_rs, gi, gis, out_p, out_d, out_i):
    NU, NI, B, S, K, C, W = dims
    T = S // NU
    PARTS = rec_rs.shape[1]
    PAIR = T // PARTS
    SEG = 2 * C // NU
    k = pl.program_id(0)

    def rows_of(g, part, which):
        out = []
        for r in range(g * 8, g * 8 + 8):
            v, t = r // T, r % T
            q = rec_r[v, t, part].astype(jnp.int32).astype(jnp.float32)
            out.append(q * rec_rs[v, t // PAIR, which : which + 1])
        return jnp.swapaxes(jnp.stack(out), 0, 1)

    for g in range(S // 8):
        out_d[:, 0, g * 8 : g * 8 + 8] = rows_of(g, pl.ds(pl.multiple_of(k * B, B), B), 0)

    @pl.when(k == K - 1)
    def _():
        for g in range(S // 8):
            out_p[:, g * 8 : g * 8 + 8] = rows_of(g, slice(B * K, B * K + B), 1)

    N = C // K
    size = min(SEG, N)
    for n in range(N // size):
        rows = slice(n * size, (n + 1) * size)
        out_i[rows] = plain(gi[rows], gis[k * N // SEG + n])


def shards(ratings, tile_mask, user_factors, item_factors, neighbours, edge_weight, dual):
    B, S, W = user_factors.shape
    K = neighbours.shape[1]
    NU = lax.axis_size("user")
    NI = lax.axis_size("item")
    C = item_factors.shape[0]
    T = S // NU
    E = B * K
    NB = B * NU
    EE = E * NU
    LOG = NU.bit_length() - 1
    ROWS = B // CHUNKS * S
    PAIR = 2 if T % 2 == 0 else 1
    PARTS = T // PAIR
    dims = (NU, NI, B, S, K, C, W)

    f32, i16, bf16 = jnp.float32, jnp.int16, jnp.bfloat16
    V = pltpu.VMEM
    dma = pltpu.SemaphoreType.DMA
    vmem = pl.BlockSpec(memory_space=pltpu.VMEM)
    hbm = pl.BlockSpec(memory_space=pltpu.HBM)
    scratch = [
        V((tile_mask.shape[1], B), jnp.int32), V((B * S, W), bf16), V((C, W), bf16), V((B, K, S, W), f32),
        V((K, NB), jnp.int32), V((K, NB), f32), dma((6,)), V((B, 1, C), f32), V((EE, 2 * NB), bf16), V((NB, 2 * EE), bf16), V((EE, W), f32),
        V((SLOTS, B // CHUNKS, S, C), bf16), V((NI, B * S, W), bf16), V((CHUNKS, ROWS, W), f32),
        V((CHUNKS, ROWS, W), f32), V((W, C), f32),
        V((NI, CHUNKS, ROWS, W), i16), V((NI, CHUNKS, 8, W), f32),
        V((NI, CHUNKS, ROWS, W), i16), V((NI, CHUNKS, 8, W), f32),
        V((S, E, W), i16), V((1, W), f32), V((NU, T, E, W), i16), V((NU, 1, W), f32),
        V((B, S, W), f32), V((S, B, W), i16), V((1, W), f32), V((NU, T, B, W), i16), V((NU, 1, W), f32),
        V((NB, PAIR * W), f32), V((NB, PAIR * W), f32), V((2 * NB, PAIR * W), bf16),
        V((EE, PAIR * W), f32), V((2 * EE, PAIR * W), bf16),
        V((NU, T, E + B, W), i16), V((PARTS, 2, W), f32),
        V((C, W), f32), V((LOG, C // 2, W), i16), V((LOG, 8, W), f32),
        V((LOG, C // 2, W), i16), V((LOG, 8, W), f32),
        dma((SLOTS,)),
        *[dma((NI, CHUNKS)) for _ in range(6)],
        *[dma((NU,)) for _ in range(4)], *[dma((NU, PARTS)) for _ in range(2)], *[dma((NU,)) for _ in range(2)],
        *[dma((NU, PARTS)) for _ in range(4)],
        *[dma((LOG,)) for _ in range(8)],
    ]
    held = pl.pallas_call(
        functools.partial(kernel, dims),
        out_shape=(
            jax.ShapeDtypeStruct((NU, T, E + B, W), i16),
            jax.ShapeDtypeStruct((NU, PARTS, 2, W), f32),
            jax.ShapeDtypeStruct((C, W), i16),
            jax.ShapeDtypeStruct((NU // 2, 8, W), f32),
        ),
        in_specs=[hbm] * 7,
        out_specs=[vmem] * 4,
        scratch_shapes=scratch,
        compiler_params=pltpu.CompilerParams(
            collective_id=0, has_side_effects=True, vmem_limit_bytes=61 << 20
        ),
        cost_estimate=pl.CostEstimate(
            flops=6 * B * S * NI * C * W, bytes_accessed=2 * B * S * NI * C, transcendentals=0
        ),
    )(
        ratings.reshape(B, NI, S, C), tile_mask.T, user_factors.reshape(B * S, W), item_factors,
        dual, neighbours.T, edge_weight.T,
    )
    return pl.pallas_call(
        functools.partial(decode, dims),
        out_shape=(
            jax.ShapeDtypeStruct((B, S, W), f32),
            jax.ShapeDtypeStruct((B, K, S, W), f32),
            jax.ShapeDtypeStruct((C, W), f32),
        ),
        grid=(K,),
        in_specs=[
            pl.BlockSpec((NU, T, E + B, W), lambda k: (0, 0, 0, 0)),
            pl.BlockSpec((NU, PARTS, 2, W), lambda k: (0, 0, 0, 0)),
            pl.BlockSpec((C // K, W), lambda k: (k, 0)),
            pl.BlockSpec((NU // 2, 8, W), lambda k: (0, 0, 0)),
        ],
        out_specs=[
            pl.BlockSpec((B, S, W), lambda k: (0, 0, 0)),
            pl.BlockSpec((B, 1, S, W), lambda k: (0, k, 0, 0)),
            pl.BlockSpec((C // K, W), lambda k: (k, 0)),
        ],
        compiler_params=pltpu.CompilerParams(vmem_limit_bytes=61 << 20),
        cost_estimate=pl.CostEstimate(
            flops=4 * B * (K + 1) * S * W, bytes_accessed=6 * B * (K + 1) * S * W, transcendentals=0
        ),
    )(*held)


def solution(mesh):
    in_specs = (
        P("user", "item"),
        P("user", "item"),
        P("user", "item", None),
        P("item", None),
        P(),
        P(),
        P("user", None, "item", None),
    )
    out_specs = (P("user", "item", None), P("user", None, "item", None), P("item", None))
    return jax.shard_map(shards, mesh=mesh, in_specs=in_specs, out_specs=out_specs, check_vma=False)
```

```python
import functools
import math

import jax
import jax.numpy as jnp
from jax import lax
from jax.experimental import pallas as pl
from jax.experimental.pallas import tpu as pltpu
from jax.sharding import PartitionSpec as P

ITERS = 2
TOP = 32767.0
TINY = 1e-30
CHUNKS = 2
LEAD = 3
SLOTS = 3
MESH = pl.DeviceIdType.MESH

descent = 0.5
dual_step = 0.5
primal_step = 0.25


def flip(index, mask, size):
    out, bit = 0, 1
    while bit < size:
        out = out + bit * lax.rem(index // bit + mask // bit, 2)
        bit *= 2
    return out


def tiles(x):
    return x.reshape(x.shape[0] // 8, 8, x.shape[1])


def peak(x):
    return jnp.max(jnp.abs(tiles(x)), axis=0)


def coded(x, inverse):
    y = tiles(x) * inverse[None]
    return jnp.round(y).astype(jnp.int32).astype(jnp.int16).reshape(x.shape)


def turned(x, inverse):
    y = jnp.swapaxes(x, 0, 1) * inverse[None]
    return jnp.round(y).astype(jnp.int32).astype(jnp.int16)


def plain(q, scale):
    y = q.astype(jnp.int32).astype(jnp.float32)
    return (tiles(y) * scale[None]).reshape(q.shape)


def steps_of(top):
    top = jnp.maximum(top, TINY)
    return TOP / top, top * (1.0 / TOP)


def kernel(
    dims, rating_ref, mask_in, user_in, item_in, dual_in, near_in, edge_in,
    rec_r, rec_rs, gi, gis,
    mask_ref, user_ref, item_ref, dual_ref, near_ref, edge_ref, load_m, own_m, seen_ref, diff_ref, back_ref, weight_ref, rat, gat, own_part, kept, total, snd_u, snd_us, rec_u, rec_us,
    snd_d, snd_ds, rec_d, rec_ds, tgt, snd_t, snd_ts, rec_t, rec_ts,
    xs, ex, hl, fl, fhl, snd_r, snd_rs,
    ired, snd_i, snd_is, rec_i, rec_is,
    rat_m, ag_s, ag_r, u_s, u_r, us_s, us_r, d_s, d_r, ds_s, ds_r, t_s, t_r, ts_s, ts_r,
    r_s, r_r, rs_s, rs_r, i_s, i_r, is_s, is_r, a_s, a_r, as_s, as_r,
):
    NU, NI, B, S, K, C, W = dims
    T = S // NU
    E = B * K
    NB = B * NU
    EE = E * NU
    LOG = NU.bit_length() - 1
    PART = B // CHUNKS
    ROWS = PART * S
    STEPS = NI * CHUNKS
    PAIR = 2 if T % 2 == 0 else 1
    PARTS = T // PAIR
    user_scale = 1.0 / math.sqrt(C * NI)
    item_scale = 1.0 / math.sqrt(B * S * NI * NU)

    u = lax.axis_index("user")
    i = lax.axis_index("item")

    def send(src, dst, s, r, device):
        return pltpu.make_async_remote_copy(
            src_ref=src, dst_ref=dst, send_sem=s, recv_sem=r, device_id=device, device_id_type=MESH
        )

    def along(d):
        return lax.rem(u + d, NU)

    def behind(d):
        return lax.rem(u + NU - d, NU)

    barrier = pltpu.get_barrier_semaphore()
    for d in range(1, NU):
        pl.semaphore_signal(barrier, inc=1, device_id=(along(d), i), device_id_type=MESH)
    for q in range(1, NI):
        pl.semaphore_signal(barrier, inc=1, device_id=(u, flip(i, q, NI)), device_id_type=MESH)

    loads = [
        pltpu.make_async_copy(src, dst, load_m.at[n])
        for n, (src, dst) in enumerate((
            (dual_in, dual_ref), (user_in, user_ref), (item_in, item_ref),
            (mask_in, mask_ref), (near_in, near_ref), (edge_in, edge_ref),
        ))
    ]
    for load in loads:
        load.start()

    EARLY = CHUNKS // 2
    FAR = (NI - 2) * CHUNKS

    def place(s):
        m = s - CHUNKS - EARLY
        p = m // CHUNKS
        far = 2 * (p // 2 + 1) + 1 - lax.rem(p, 2)
        q = jnp.where(s < CHUNKS, 0, jnp.where((m < 0) | (m >= FAR), 1, far))
        c = jnp.where(m < 0, lax.rem(s, CHUNKS), lax.rem(m, CHUNKS))
        c = jnp.where(m >= FAR, m - FAR + EARLY, c)
        return c, q

    def fetch(s):
        c, q = place(s)
        slot = lax.rem(s, SLOTS)
        return pltpu.make_async_copy(
            rating_ref.at[pl.ds(c * PART, PART), flip(i, q, NI)], rat.at[slot], rat_m.at[slot]
        )

    for s in range(SLOTS - 1):
        fetch(jnp.int32(s)).start()

    def gather(q, c):
        rows = pl.ds(pl.multiple_of(c * ROWS, ROWS), ROWS)
        return send(
            user_ref.at[rows], gat.at[q, rows], ag_s.at[q, c], ag_r.at[q, c], (u, flip(i, q, NI))
        )

    def pass_on(q, c):
        rows = pl.ds(pl.multiple_of(c * ROWS, ROWS), ROWS)
        return send(
            gat.at[q, rows], gat.at[q + 1, rows], ag_s.at[q + 1, c], ag_r.at[q + 1, c],
            (u, flip(i, 1, NI)),
        )

    def give_user(q, c):
        to = q * (1 - lax.rem(q, 2)) + lax.rem(q, 2)
        device = (u, flip(i, to, NI))
        return (
            send(snd_u.at[q, c], rec_u.at[q, c], u_s.at[q, c], u_r.at[q, c], device),
            send(snd_us.at[q, c], rec_us.at[q, c], us_s.at[q, c], us_r.at[q, c], device),
        )

    def gradient(s, _):
        c, q = place(s)
        slot = lax.rem(s, SLOTS)

        @pl.when(s + SLOTS - 1 < STEPS)
        def _():
            fetch(s + SLOTS - 1).start()

        if NI > 2:
            m = s - CHUNKS
            ahead = 2 * (m // (2 * CHUNKS) + 1)
            which = lax.rem(m, 2 * CHUNKS)

            @pl.when((m >= 0) & (ahead < NI) & (which < CHUNKS))
            def _():
                gather(ahead, which).wait_recv()
                pass_on(ahead, which).start()

        fetch(s).wait()

        @pl.when(lax.rem(q, 2) == 1)
        def _():
            gather(q, c).wait_recv()

        users = gat[q, pl.ds(pl.multiple_of(c * ROWS, ROWS), ROWS)]
        items = item_ref[...]
        scores = lax.dot_general(
            users, items, (((1,), (1,)), ((), ())), preferred_element_type=jnp.float32
        )
        error = scores.reshape(PART, S, C) - rat[slot].astype(jnp.float32)
        error = (seen_ref[pl.ds(c * PART, PART)] * error).astype(jnp.bfloat16).reshape(ROWS, C)
        total[...] += jnp.dot(users.T, error, preferred_element_type=jnp.float32)
        own_part[c] = jnp.dot(error, items, preferred_element_type=jnp.float32)

        @pl.when(q > 0)
        def _():
            @pl.when(lax.rem(q, 2) == 0)
            def _():
                for copy in give_user(q + 1, c):
                    copy.wait_recv()
                own_part[c] += plain(rec_u[q + 1, c], rec_us[q + 1, c])

            term = own_part[c]
            inverse, scale = steps_of(peak(term))
            snd_u[q, c] = coded(term, inverse)
            snd_us[q, c] = scale
            for copy in give_user(q, c):
                copy.start()

        @pl.when(q == 0)
        def _():
            kept[c] = own_part[c]

        return 0

    loads[0].wait()
    top = lax.fori_loop(
        0, B,
        lambda b, m: jnp.maximum(m, peak(dual_ref[b].reshape(K * S, W))),
        jnp.zeros((8, W), jnp.float32),
    )
    dual_inverse, dual_scale = steps_of(jnp.max(top, axis=0, keepdims=True))
    snd_ds[...] = dual_scale

    pl.semaphore_wait(barrier, NU - 1 + NI - 1)

    def give_dual(d):
        rows = pl.ds(along(d) * T, T)
        return send(snd_d.at[rows], rec_d.at[u], d_s.at[d], d_r.at[d], (along(d), i))

    def give_step(d):
        return send(snd_ds, rec_ds.at[u], ds_s.at[d], ds_r.at[d], (along(d), i))

    def turn_dual(g):
        rows = pl.ds(pl.multiple_of(g * 8, 8), 8)
        for k in range(K):
            snd_d[rows, k * B : (k + 1) * B] = turned(dual_ref[:, k, rows, :], dual_inverse)

    if T % 8:
        for g in range(S // 8):
            turn_dual(g)
    for d in range(1, NU):
        if T % 8 == 0:
            for g in range(T // 8):
                turn_dual(along(d) * (T // 8) + g)
        give_dual(d).start()

    for load in loads[1:]:
        load.wait()
    for c in range(CHUNKS):
        for q in range(2, NI, 2):
            gather(q, c).start()
        gather(1, c).start()
    for d in range(1, NU):
        give_step(d).start()
    if T % 8 == 0:
        for g in range(T // 8):
            turn_dual(u * (T // 8) + g)

    spread = lax.broadcasted_iota(jnp.int32, (mask_ref.shape[0], C), 1) // (C // mask_ref.shape[0])
    spread = jnp.where(spread == lax.broadcasted_iota(jnp.int32, spread.shape, 0), 1.0, 0.0)
    seen = lax.dot_general(
        mask_ref[...].astype(jnp.float32), spread, (((0,), (0,)), ((), ())),
        preferred_element_type=jnp.float32,
    )
    for b in range(B):
        seen_ref[b] = seen[b : b + 1]
    gat[0] = user_ref[...]
    total[...] = jnp.zeros_like(total)
    lax.fori_loop(0, STEPS, gradient, 0)

    rec_d[u] = snd_d[pl.ds(u * T, T)]
    rec_ds[u] = dual_scale

    def half(s):
        h = C >> (s + 1)
        base = 0
        for t in range(s):
            base = base + lax.rem(u // (1 << t), 2) * (C >> (t + 1))
        bit = lax.rem(u // (1 << s), 2)
        keep = pl.ds(pl.multiple_of(base + bit * h, h), h)
        away = pl.ds(pl.multiple_of(base + (1 - bit) * h, h), h)
        return keep, away, h

    def partner(s):
        return (flip(u, 1 << s, NU), i)

    LAST = LOG - 1

    def give_item(s):
        h = C >> min(s + 1, LAST)
        return (
            send(snd_i.at[s, pl.ds(0, h)], rec_i.at[s, pl.ds(0, h)], i_s.at[s], i_r.at[s], partner(s)),
            send(snd_is.at[s], rec_is.at[s], is_s.at[s], is_r.at[s], partner(s)),
        )

    def halve_send(s):
        if s < LAST:
            _, away, h = half(s)
        else:
            away, _, h = half(LAST - 1)
        part = ired[away]
        inverse, scale = steps_of(peak(part))
        snd_i[s, pl.ds(0, h)] = coded(part, inverse)
        snd_is[s] = scale
        if s == LAST:
            ired[away] = plain(snd_i[s, pl.ds(0, h)], scale)
        for copy in give_item(s):
            copy.start()

    def halve_take(s):
        keep, _, h = half(min(s, LAST - 1))
        for copy in give_item(s):
            copy.wait_recv()
        ired[keep] += plain(rec_i[s, pl.ds(0, h)], rec_is[s])

    SEG = C >> LAST

    def give_all(s):
        keep, _, h = half(s)
        n = h // SEG
        base = 0
        for t in range(s + 1):
            base = base + lax.rem(u // (1 << t), 2) * ((C >> (t + 1)) // SEG)
        tile = pl.ds(base, n)
        return (
            send(gi.at[keep], gi.at[keep], a_s.at[s], a_r.at[s], partner(s)),
            send(gis.at[tile], gis.at[tile], as_s.at[s], as_r.at[s], partner(s)),
        )

    def double_first():
        keep, _, _ = half(LAST - 1)
        base = 0
        for t in range(LAST):
            base = base + lax.rem(u // (1 << t), 2) * (NU >> (t + 2))
        part = ired[keep]
        inverse, scale = steps_of(peak(part))
        gi[keep] = coded(part, inverse)
        gis[base] = scale

    def double_send(s):
        for copy in give_all(s):
            copy.start()

    def double_take(s):
        for copy in give_all(s):
            copy.wait_recv()

    def close(c, m):
        g = kept[c]
        for q in [*range(2, NI, 2), 1]:
            for copy in give_user(q, c):
                copy.wait_recv()
            g = g + plain(rec_u[q, c], rec_us[q, c])
        rows = pl.ds(pl.multiple_of(c * ROWS, ROWS), ROWS)
        t = user_ref[rows].astype(jnp.float32) - (descent * user_scale) * g
        tgt[pl.ds(c * PART, PART)] = t.reshape(PART, S, W)
        return jnp.maximum(m, peak(t))

    top = lax.fori_loop(0, CHUNKS, close, jnp.zeros((8, W), jnp.float32))
    target_inverse, target_scale = steps_of(jnp.max(top, axis=0, keepdims=True))
    snd_ts[...] = target_scale

    def turn_target(g, _):
        rows = pl.ds(pl.multiple_of(g * 8, 8), 8)
        snd_t[rows] = turned(tgt[:, rows, :], target_inverse)
        return 0

    lax.fori_loop(0, S // 8, turn_target, 0)

    def give_scale(d):
        return send(snd_ts, rec_ts.at[u], ts_s.at[d], ts_r.at[d], (along(d), i))

    def give_target(d, ch):
        return send(
            snd_t.at[pl.ds(along(d) * T + ch * PAIR, PAIR)], rec_t.at[u, pl.ds(ch * PAIR, PAIR)],
            t_s.at[d, ch], t_r.at[d, ch], (along(d), i),
        )

    for d in range(1, NU):
        give_scale(d).start()
    for ch in range(PARTS):
        for d in range(1, NU):
            give_target(d, ch).start()
    ired[...] = total[...].T * item_scale
    halve_send(0)
    rec_t[u] = snd_t[pl.ds(u * T, T)]
    rec_ts[u] = target_scale

    down = lax.broadcasted_iota(jnp.int32, (NB, NB), 0)
    across = lax.broadcasted_iota(jnp.int32, (NB, NB), 1)
    for k in range(K):
        rows = slice(k * NB, (k + 1) * NB)
        again = slice(EE + k * NB, EE + (k + 1) * NB)
        m = jnp.where(down == across, 1.0, 0.0) - jnp.where(down == near_ref[k : k + 1], 1.0, 0.0)
        side = m.T.astype(jnp.bfloat16)
        back_ref[:, rows] = m.astype(jnp.bfloat16)
        back_ref[:, again] = m.astype(jnp.bfloat16)
        diff_ref[rows, :NB] = side
        diff_ref[rows, NB:] = side
        weight_ref[rows] = jnp.broadcast_to(edge_ref[k : k + 1], (W, NB)).T

    chain = iter(range(LOG + LAST))

    def item_step():
        s = next(chain, None)
        if s is None:
            return
        if s < LOG:
            halve_take(s)
            if s < LAST:
                halve_send(s + 1)
            else:
                double_first()
                double_send(LAST - 1)
        else:
            s = LOG + LAST - 1 - s
            double_take(s)
            if s > 0:
                double_send(s - 1)

    for d in range(1, NU):
        give_dual(d).wait_recv()
        give_step(d).wait_recv()
    for d in range(1, NU):
        give_scale(d).wait_recv()

    GROUP = 128

    def split(x):
        high = x.astype(jnp.bfloat16)
        return high, (x - high.astype(jnp.float32)).astype(jnp.bfloat16)

    def give_result(d, ch):
        device = (along(d), i)
        rows = pl.ds(ch * PAIR, PAIR)
        return (
            send(snd_r.at[along(d), rows], rec_r.at[u, rows], r_s.at[d, ch], r_r.at[d, ch], device),
            send(snd_rs.at[ch], rec_rs.at[u, ch], rs_s.at[d, ch], rs_r.at[d, ch], device),
        )

    def fold(m):
        m = jnp.max(m, axis=0, keepdims=True)
        out = m[:, :W]
        for n in range(1, PAIR):
            out = jnp.maximum(out, m[:, n * W : (n + 1) * W])
        return out

    CUT = NU // 2

    def own_result(ch):
        rows = pl.ds(ch * PAIR, PAIR)
        return pltpu.make_async_copy(snd_r.at[u, rows], rec_r.at[u, rows], own_m.at[ch])

    def unit(n):
        return n // 2, range(1, CUT) if n % 2 == 0 else range(CUT, NU)

    def unit_start(n):
        ch, ds = unit(n)
        for d in ds:
            for copy in give_result(d, ch):
                copy.start()

    def unit_wait(n):
        ch, ds = unit(n)
        for d in ds:
            for copy in give_result(d, ch):
                copy.wait_recv()

    def sweep_rows(ch, _):
        for d in range(1, NU):
            give_target(d, ch).wait_recv()
        for n in range(PAIR):
            r = ch * PAIR + n
            lanes = slice(n * W, (n + 1) * W)
            for v in range(NU):
                xs[v * B : (v + 1) * B, lanes] = plain(rec_t[v, r], rec_ts[v])
                flux = plain(rec_d[v, r], rec_ds[v])
                for k in range(K):
                    fl[k * NB + v * B : k * NB + (v + 1) * B, lanes] = flux[k * B : (k + 1) * B]

        peaks = None
        for sweep in range(ITERS):
            source = xs[...] if sweep == 0 else ex[...]
            hl[:NB], hl[NB:] = split(source)
            peaks = jnp.zeros((8, PAIR * W), jnp.float32)
            for g in range(0, EE, GROUP):
                rows = slice(g, g + GROUP)
                slope = jnp.dot(diff_ref[rows], hl[...], preferred_element_type=jnp.float32)
                moved = fl[rows] + dual_step * slope
                w = weight_ref[rows]
                parts = []
                for n in range(PAIR):
                    m = moved[:, n * W : (n + 1) * W]
                    square = jnp.sum(m * m, axis=-1, keepdims=True)
                    parts.append(m * (w * lax.rsqrt(jnp.maximum(square, w * w))))
                flux = jnp.concatenate(parts, axis=1) if PAIR > 1 else parts[0]
                fl[rows] = flux
                fhl[rows], fhl[EE + g : EE + g + GROUP] = split(flux)
                peaks = jnp.maximum(peaks, peak(flux))
            div = jnp.dot(back_ref[...], fhl[...], preferred_element_type=jnp.float32)
            target = xs[...]
            if sweep == 0:
                primal = target
            newer = (primal - primal_step * div + primal_step * target) / (1.0 + primal_step)
            if sweep < ITERS - 1:
                ex[...] = 2.0 * newer - primal
            primal = newer

        flux_inverse, flux_scale = steps_of(fold(peaks))
        primal_inverse, primal_scale = steps_of(fold(peak(primal)))
        scales = jnp.concatenate([flux_scale, primal_scale], axis=0)
        snd_rs[ch] = scales
        for n in range(PAIR):
            r = ch * PAIR + n
            lanes = slice(n * W, (n + 1) * W)
            for v in range(NU):
                for k in range(K):
                    part = fl[k * NB + v * B : k * NB + (v + 1) * B, lanes]
                    snd_r[v, r, k * B : (k + 1) * B] = coded(part, flux_inverse)
                snd_r[v, r, E:] = coded(primal[v * B : (v + 1) * B, lanes], primal_inverse)
        own_result(ch).start()
        rec_rs[u, ch] = scales

        for n in range(min(LEAD, 2 * PARTS)):
            @pl.when(ch == n // 2)
            def _():
                if n == 2:
                    item_step()
                unit_start(n)

        return 0

    lax.fori_loop(0, PARTS, sweep_rows, 0)

    for n in range(2 * PARTS):
        unit_wait(n)
        if n % 2 == 0:
            item_step()
        if n + LEAD < 2 * PARTS:
            unit_start(n + LEAD)
    for _ in range(2 * LOG):
        item_step()

    for ch in range(PARTS):
        own_result(ch).wait()
    for q in range(1, NI):
        for c in range(CHUNKS):
            (pass_on(q - 1, c) if q > 1 and q % 2 else gather(q, c)).wait_send()
            for copy in give_user(q, c):
                copy.wait_send()
    for d in range(1, NU):
        for copy in (give_dual(d), give_step(d), give_scale(d)):
            copy.wait_send()
        for ch in range(PARTS):
            give_target(d, ch).wait_send()
            for copy in give_result(d, ch):
                copy.wait_send()
    for s in range(LOG):
        for copy in give_item(s) + (give_all(s) if s < LAST else ()):
            copy.wait_send()


def decode(dims, rec_in, recs_in, gi_in, gis_in, out_p, out_d, out_i, rec_r, rec_rs, gi, gis, op, od, oi, load_m, save_m):
    NU, NI, B, S, K, C, W = dims
    T = S // NU
    PAIR = T // rec_rs.shape[1]
    SEG = C // gis.shape[0]
    parts = [pl.ds(k * B, B) for k in range(K + 1)]
    loads = [
        pltpu.make_async_copy(src, dst, load_m.at[n])
        for n, (src, dst) in enumerate([
            (recs_in, rec_rs), (gis_in, gis), (gi_in, gi),
            *[(rec_in.at[:, :, p], rec_r.at[:, :, p]) for p in parts],
        ])
    ]
    for load in loads:
        load.start()

    def save(n, src, dst):
        copy = pltpu.make_async_copy(src, dst, save_m.at[n])
        copy.start()
        return copy

    def rows_of(g, k, which):
        out = []
        for r in range(g * 8, g * 8 + 8):
            v, t = r // T, r % T
            q = rec_r[v, t, k * B : (k + 1) * B].astype(jnp.int32).astype(jnp.float32)
            out.append(q * rec_rs[v, t // PAIR, which : which + 1])
        return jnp.swapaxes(jnp.stack(out), 0, 1)

    for load in loads[:3]:
        load.wait()
    saves = []
    for n in range(gis.shape[0]):
        rows = slice(n * SEG, (n + 1) * SEG)
        oi[rows] = plain(gi[rows], gis[n])
    saves.append(save(K + 1, oi, out_i))
    for k in range(K):
        loads[3 + k].wait()
        for g in range(S // 8):
            od[:, k, g * 8 : g * 8 + 8] = rows_of(g, k, 0)
        saves.append(save(k, od.at[:, k], out_d.at[:, k]))
    loads[3 + K].wait()
    for g in range(S // 8):
        op[:, g * 8 : g * 8 + 8] = rows_of(g, K, 1)
    saves.append(save(K, op, out_p))
    for copy in saves:
        copy.wait()


def shards(ratings, tile_mask, user_factors, item_factors, neighbours, edge_weight, dual):
    B, S, W = user_factors.shape
    K = neighbours.shape[1]
    NU = lax.axis_size("user")
    NI = lax.axis_size("item")
    C = item_factors.shape[0]
    T = S // NU
    E = B * K
    NB = B * NU
    EE = E * NU
    LOG = NU.bit_length() - 1
    ROWS = B // CHUNKS * S
    PAIR = 2 if T % 2 == 0 else 1
    PARTS = T // PAIR
    dims = (NU, NI, B, S, K, C, W)

    f32, i16, bf16 = jnp.float32, jnp.int16, jnp.bfloat16
    V = pltpu.VMEM
    dma = pltpu.SemaphoreType.DMA
    vmem = pl.BlockSpec(memory_space=pltpu.VMEM)
    hbm = pl.BlockSpec(memory_space=pltpu.HBM)
    scratch = [
        V((tile_mask.shape[1], B), jnp.int32), V((B * S, W), bf16), V((C, W), bf16), V((B, K, S, W), f32),
        V((K, NB), jnp.int32), V((K, NB), f32), dma((6,)), dma((PARTS,)), V((B, 1, C), f32), V((EE, 2 * NB), bf16), V((NB, 2 * EE), bf16), V((EE, W), f32),
        V((SLOTS, B // CHUNKS, S, C), bf16), V((NI, B * S, W), bf16), V((CHUNKS, ROWS, W), f32),
        V((CHUNKS, ROWS, W), f32), V((W, C), f32),
        V((NI, CHUNKS, ROWS, W), i16), V((NI, CHUNKS, 8, W), f32),
        V((NI, CHUNKS, ROWS, W), i16), V((NI, CHUNKS, 8, W), f32),
        V((S, E, W), i16), V((1, W), f32), V((NU, T, E, W), i16), V((NU, 1, W), f32),
        V((B, S, W), f32), V((S, B, W), i16), V((1, W), f32), V((NU, T, B, W), i16), V((NU, 1, W), f32),
        V((NB, PAIR * W), f32), V((NB, PAIR * W), f32), V((2 * NB, PAIR * W), bf16),
        V((EE, PAIR * W), f32), V((2 * EE, PAIR * W), bf16),
        V((NU, T, E + B, W), i16), V((PARTS, 2, W), f32),
        V((C, W), f32), V((LOG, C // 2, W), i16), V((LOG, 8, W), f32),
        V((LOG, C // 2, W), i16), V((LOG, 8, W), f32),
        dma((SLOTS,)),
        *[dma((NI, CHUNKS)) for _ in range(6)],
        *[dma((NU,)) for _ in range(4)], *[dma((NU, PARTS)) for _ in range(2)], *[dma((NU,)) for _ in range(2)],
        *[dma((NU, PARTS)) for _ in range(4)],
        *[dma((LOG,)) for _ in range(8)],
    ]
    held = pl.pallas_call(
        functools.partial(kernel, dims),
        out_shape=(
            jax.ShapeDtypeStruct((NU, T, E + B, W), i16),
            jax.ShapeDtypeStruct((NU, PARTS, 2, W), f32),
            jax.ShapeDtypeStruct((C, W), i16),
            jax.ShapeDtypeStruct((NU // 2, 8, W), f32),
        ),
        in_specs=[hbm] * 7,
        out_specs=[pl.BlockSpec(memory_space=pl.ANY)] + [vmem] * 3,
        scratch_shapes=scratch,
        compiler_params=pltpu.CompilerParams(
            collective_id=0, has_side_effects=True, vmem_limit_bytes=61 << 20
        ),
        cost_estimate=pl.CostEstimate(
            flops=6 * B * S * NI * C * W, bytes_accessed=2 * B * S * NI * C, transcendentals=0
        ),
    )(
        ratings.reshape(B, NI, S, C), tile_mask.T, user_factors.reshape(B * S, W), item_factors,
        dual, neighbours.T, edge_weight.T,
    )
    return pl.pallas_call(
        functools.partial(decode, dims),
        out_shape=(
            jax.ShapeDtypeStruct((B, S, W), f32),
            jax.ShapeDtypeStruct((B, K, S, W), f32),
            jax.ShapeDtypeStruct((C, W), f32),
        ),
        in_specs=[hbm] * 4,
        out_specs=[hbm] * 3,
        scratch_shapes=[
            V((NU, T, E + B, W), i16), V((NU, PARTS, 2, W), f32), V((C, W), i16), V((NU // 2, 8, W), f32),
            V((B, S, W), f32), V((B, K, S, W), f32), V((C, W), f32), dma((K + 4,)), dma((K + 2,)),
        ],
        compiler_params=pltpu.CompilerParams(vmem_limit_bytes=61 << 20),
        cost_estimate=pl.CostEstimate(
            flops=4 * B * (K + 1) * S * W, bytes_accessed=6 * B * (K + 1) * S * W, transcendentals=0
        ),
    )(*held)


def solution(mesh):
    in_specs = (
        P("user", "item"),
        P("user", "item"),
        P("user", "item", None),
        P("item", None),
        P(),
        P(),
        P("user", None, "item", None),
    )
    out_specs = (P("user", "item", None), P("user", None, "item", None), P("item", None))
    return jax.shard_map(shards, mesh=mesh, in_specs=in_specs, out_specs=out_specs, check_vma=False)
```

```python
import functools
import math

import jax
import jax.numpy as jnp
from jax import lax
from jax.experimental import pallas as pl
from jax.experimental.pallas import tpu as pltpu
from jax.sharding import PartitionSpec as P

ITERS = 2
TOP = 32767.0
TINY = 1e-30
CHUNKS = 2
LEAD = 3
SLOTS = 3
MESH = pl.DeviceIdType.MESH

descent = 0.5
dual_step = 0.5
primal_step = 0.25


def flip(index, mask, size):
    out, bit = 0, 1
    while bit < size:
        out = out + bit * lax.rem(index // bit + mask // bit, 2)
        bit *= 2
    return out


def tiles(x):
    return x.reshape(x.shape[0] // 8, 8, x.shape[1])


def peak(x):
    return jnp.max(jnp.abs(tiles(x)), axis=0)


def coded(x, inverse):
    y = tiles(x) * inverse[None]
    return jnp.round(y).astype(jnp.int32).astype(jnp.int16).reshape(x.shape)


def turned(x, inverse):
    y = jnp.swapaxes(x, 0, 1) * inverse[None]
    return jnp.round(y).astype(jnp.int32).astype(jnp.int16)


def plain(q, scale):
    y = q.astype(jnp.int32).astype(jnp.float32)
    return (tiles(y) * scale[None]).reshape(q.shape)


def steps_of(top):
    top = jnp.maximum(top, TINY)
    return TOP / top, top * (1.0 / TOP)


def kernel(
    dims, rating_ref, mask_in, user_in, item_in, dual_in, near_in, edge_in,
    rec_r, rec_rs, gi, gis,
    mask_ref, user_ref, item_ref, dual_ref, near_ref, edge_ref, load_m, own_m, dual_m, seen_ref, diff_ref, back_ref, weight_ref, rat, gat, own_part, kept, total, snd_u, snd_us, rec_u, rec_us,
    snd_d, snd_ds, rec_d, rec_ds, tgt, snd_t, snd_ts, rec_t, rec_ts,
    xs, ex, hl, fl, fhl, snd_r, snd_rs,
    ired, snd_i, snd_is, rec_i, rec_is,
    rat_m, ag_s, ag_r, u_s, u_r, us_s, us_r, d_s, d_r, ds_s, ds_r, t_s, t_r, ts_s, ts_r,
    r_s, r_r, rs_s, rs_r, i_s, i_r, is_s, is_r, a_s, a_r, as_s, as_r,
):
    NU, NI, B, S, K, C, W = dims
    T = S // NU
    E = B * K
    NB = B * NU
    EE = E * NU
    LOG = NU.bit_length() - 1
    PART = B // CHUNKS
    ROWS = PART * S
    STEPS = NI * CHUNKS
    PAIR = 2 if T % 2 == 0 else 1
    PARTS = T // PAIR
    user_scale = 1.0 / math.sqrt(C * NI)
    item_scale = 1.0 / math.sqrt(B * S * NI * NU)

    u = lax.axis_index("user")
    i = lax.axis_index("item")

    def send(src, dst, s, r, device):
        return pltpu.make_async_remote_copy(
            src_ref=src, dst_ref=dst, send_sem=s, recv_sem=r, device_id=device, device_id_type=MESH
        )

    def along(d):
        return lax.rem(u + d, NU)

    def behind(d):
        return lax.rem(u + NU - d, NU)

    barrier = pltpu.get_barrier_semaphore()
    for d in range(1, NU):
        pl.semaphore_signal(barrier, inc=1, device_id=(along(d), i), device_id_type=MESH)
    for q in range(1, NI):
        pl.semaphore_signal(barrier, inc=1, device_id=(u, flip(i, q, NI)), device_id_type=MESH)

    loads = [
        pltpu.make_async_copy(src, dst, load_m.at[n])
        for n, (src, dst) in enumerate((
            (user_in, user_ref), (item_in, item_ref),
            (mask_in, mask_ref), (near_in, near_ref), (edge_in, edge_ref),
        ))
    ]

    GR = max(T, 8)
    ORDER = [along(d) * T // GR for d in range(1, NU)] + [u * T // GR] if GR == T else list(range(S // GR))

    def load_dual(g):
        rows = pl.ds(pl.multiple_of(g * GR, GR), GR)
        return pltpu.make_async_copy(dual_in.at[:, :, rows], dual_ref.at[:, :, rows], dual_m.at[g])

    for g in ORDER:
        load_dual(g).start()
    for load in loads:
        load.start()

    EARLY = CHUNKS // 2
    LATE = CHUNKS - EARLY
    FAR = (NI - 2) * CHUNKS

    def place(s):
        m = s - 2 * EARLY
        k = lax.rem(m, 2 * CHUNKS)
        r = m - FAR
        q = jnp.where(m < FAR, 2 * (m // (2 * CHUNKS) + 1) + 1 - lax.rem(k, 2), jnp.where(r < LATE, 1, 0))
        c = jnp.where(m < FAR, k // 2, jnp.where(r < LATE, EARLY + r, EARLY + r - LATE))
        q = jnp.where(m < 0, s // EARLY, q)
        c = jnp.where(m < 0, lax.rem(s, EARLY), c)
        return c, q

    def fetch(s):
        c, q = place(s)
        slot = lax.rem(s, SLOTS)
        return pltpu.make_async_copy(
            rating_ref.at[pl.ds(c * PART, PART), flip(i, q, NI)], rat.at[slot], rat_m.at[slot]
        )

    for s in range(SLOTS - 1):
        fetch(jnp.int32(s)).start()

    def gather(q, c):
        rows = pl.ds(pl.multiple_of(c * ROWS, ROWS), ROWS)
        return send(
            user_ref.at[rows], gat.at[q, rows], ag_s.at[q, c], ag_r.at[q, c], (u, flip(i, q, NI))
        )

    def pass_on(q, c):
        rows = pl.ds(pl.multiple_of(c * ROWS, ROWS), ROWS)
        return send(
            gat.at[q, rows], gat.at[q + 1, rows], ag_s.at[q + 1, c], ag_r.at[q + 1, c],
            (u, flip(i, 1, NI)),
        )

    def give_user(q, c):
        to = q * (1 - lax.rem(q, 2)) + lax.rem(q, 2)
        device = (u, flip(i, to, NI))
        return (
            send(snd_u.at[q, c], rec_u.at[q, c], u_s.at[q, c], u_r.at[q, c], device),
            send(snd_us.at[q, c], rec_us.at[q, c], us_s.at[q, c], us_r.at[q, c], device),
        )

    def gradient(s, _):
        c, q = place(s)
        slot = lax.rem(s, SLOTS)

        @pl.when(s + SLOTS - 1 < STEPS)
        def _():
            fetch(s + SLOTS - 1).start()

        if NI > 2:
            m = s - 2 * EARLY
            ahead = 2 * (m // (2 * CHUNKS) + 1)
            k = lax.rem(m, 2 * CHUNKS)

            @pl.when((m >= 0) & (m < FAR) & ((k == 0) | ((lax.rem(k, 2) == 1) & (k < 2 * CHUNKS - 1))))
            def _():
                gather(ahead, (k + 1) // 2).wait_recv()
                pass_on(ahead, (k + 1) // 2).start()

        fetch(s).wait()

        @pl.when(lax.rem(q, 2) == 1)
        def _():
            gather(q, c).wait_recv()

        users = gat[q, pl.ds(pl.multiple_of(c * ROWS, ROWS), ROWS)]
        items = item_ref[...]
        scores = lax.dot_general(
            users, items, (((1,), (1,)), ((), ())), preferred_element_type=jnp.float32
        )
        error = scores.reshape(PART, S, C) - rat[slot].astype(jnp.float32)
        error = (seen_ref[pl.ds(c * PART, PART)] * error).astype(jnp.bfloat16).reshape(ROWS, C)
        total[...] += jnp.dot(users.T, error, preferred_element_type=jnp.float32)
        own_part[c] = jnp.dot(error, items, preferred_element_type=jnp.float32)

        @pl.when(q > 0)
        def _():
            @pl.when(lax.rem(q, 2) == 0)
            def _():
                for copy in give_user(q + 1, c):
                    copy.wait_recv()
                own_part[c] += plain(rec_u[q + 1, c], rec_us[q + 1, c])

            term = own_part[c]
            inverse, scale = steps_of(peak(term))
            snd_u[q, c] = coded(term, inverse)
            snd_us[q, c] = scale
            for copy in give_user(q, c):
                copy.start()

        @pl.when(q == 0)
        def _():
            kept[c] = own_part[c]

        return 0

    pl.semaphore_wait(barrier, NU - 1 + NI - 1)

    def give_dual(d):
        rows = pl.ds(along(d) * T, T)
        return send(snd_d.at[rows], rec_d.at[u], d_s.at[d], d_r.at[d], (along(d), i))

    def give_step(d):
        return send(snd_ds.at[along(d) * T // GR], rec_ds.at[u], ds_s.at[d], ds_r.at[d], (along(d), i))

    def turn_dual(g):
        load_dual(g).wait()
        top = jnp.zeros((8, W), jnp.float32)
        for h in range(GR // 8):
            rows = pl.ds(pl.multiple_of(g * GR + h * 8, 8), 8)
            top = jnp.maximum(top, peak(dual_ref[:, :, rows, :].reshape(E * 8, W)))
        inverse, scale = steps_of(jnp.max(top, axis=0, keepdims=True))
        snd_ds[g] = scale
        for h in range(GR // 8):
            rows = pl.ds(pl.multiple_of(g * GR + h * 8, 8), 8)
            for k in range(K):
                snd_d[rows, k * B : (k + 1) * B] = turned(dual_ref[:, k, rows, :], inverse)

    if GR > T:
        for g in ORDER:
            turn_dual(g)
    for d in range(1, NU):
        if GR == T:
            turn_dual(ORDER[d - 1])
        give_dual(d).start()

    for load in loads:
        load.wait()
    for c in range(CHUNKS):
        for q in range(2, NI, 2):
            gather(q, c).start()
        gather(1, c).start()
    for d in range(1, NU):
        give_step(d).start()
    if GR == T:
        turn_dual(ORDER[NU - 1])

    spread = lax.broadcasted_iota(jnp.int32, (mask_ref.shape[0], C), 1) // (C // mask_ref.shape[0])
    spread = jnp.where(spread == lax.broadcasted_iota(jnp.int32, spread.shape, 0), 1.0, 0.0)
    seen = lax.dot_general(
        mask_ref[...].astype(jnp.float32), spread, (((0,), (0,)), ((), ())),
        preferred_element_type=jnp.float32,
    )
    for b in range(B):
        seen_ref[b] = seen[b : b + 1]
    gat[0] = user_ref[...]
    total[...] = jnp.zeros_like(total)
    lax.fori_loop(0, STEPS, gradient, 0)

    rec_d[u] = snd_d[pl.ds(u * T, T)]
    rec_ds[u] = snd_ds[u * T // GR]

    def half(s):
        h = C >> (s + 1)
        base = 0
        for t in range(s):
            base = base + lax.rem(u // (1 << t), 2) * (C >> (t + 1))
        bit = lax.rem(u // (1 << s), 2)
        keep = pl.ds(pl.multiple_of(base + bit * h, h), h)
        away = pl.ds(pl.multiple_of(base + (1 - bit) * h, h), h)
        return keep, away, h

    def partner(s):
        return (flip(u, 1 << s, NU), i)

    LAST = LOG - 1

    def give_item(s):
        h = C >> min(s + 1, LAST)
        return (
            send(snd_i.at[s, pl.ds(0, h)], rec_i.at[s, pl.ds(0, h)], i_s.at[s], i_r.at[s], partner(s)),
            send(snd_is.at[s], rec_is.at[s], is_s.at[s], is_r.at[s], partner(s)),
        )

    def halve_send(s):
        if s < LAST:
            _, away, h = half(s)
        else:
            away, _, h = half(LAST - 1)
        part = ired[away]
        inverse, scale = steps_of(peak(part))
        snd_i[s, pl.ds(0, h)] = coded(part, inverse)
        snd_is[s] = scale
        if s == LAST:
            ired[away] = plain(snd_i[s, pl.ds(0, h)], scale)
        for copy in give_item(s):
            copy.start()

    def halve_take(s):
        keep, _, h = half(min(s, LAST - 1))
        for copy in give_item(s):
            copy.wait_recv()
        ired[keep] += plain(rec_i[s, pl.ds(0, h)], rec_is[s])

    SEG = C >> LAST

    def give_all(s):
        keep, _, h = half(s)
        n = h // SEG
        base = 0
        for t in range(s + 1):
            base = base + lax.rem(u // (1 << t), 2) * ((C >> (t + 1)) // SEG)
        tile = pl.ds(base, n)
        return (
            send(gi.at[keep], gi.at[keep], a_s.at[s], a_r.at[s], partner(s)),
            send(gis.at[tile], gis.at[tile], as_s.at[s], as_r.at[s], partner(s)),
        )

    def double_first():
        keep, _, _ = half(LAST - 1)
        base = 0
        for t in range(LAST):
            base = base + lax.rem(u // (1 << t), 2) * (NU >> (t + 2))
        part = ired[keep]
        inverse, scale = steps_of(peak(part))
        gi[keep] = coded(part, inverse)
        gis[base] = scale

    def double_send(s):
        for copy in give_all(s):
            copy.start()

    def double_take(s):
        for copy in give_all(s):
            copy.wait_recv()

    def close(c, m):
        g = kept[c]
        for q in [*range(2, NI, 2), 1]:
            for copy in give_user(q, c):
                copy.wait_recv()
            g = g + plain(rec_u[q, c], rec_us[q, c])
        rows = pl.ds(pl.multiple_of(c * ROWS, ROWS), ROWS)
        t = user_ref[rows].astype(jnp.float32) - (descent * user_scale) * g
        tgt[pl.ds(c * PART, PART)] = t.reshape(PART, S, W)
        return jnp.maximum(m, peak(t))

    top = lax.fori_loop(0, CHUNKS, close, jnp.zeros((8, W), jnp.float32))
    target_inverse, target_scale = steps_of(jnp.max(top, axis=0, keepdims=True))
    snd_ts[...] = target_scale

    def turn_target(g, _):
        rows = pl.ds(pl.multiple_of(g * 8, 8), 8)
        snd_t[rows] = turned(tgt[:, rows, :], target_inverse)
        return 0

    lax.fori_loop(0, S // 8, turn_target, 0)

    def give_scale(d):
        return send(snd_ts, rec_ts.at[u], ts_s.at[d], ts_r.at[d], (along(d), i))

    def give_target(d, ch):
        return send(
            snd_t.at[pl.ds(along(d) * T + ch * PAIR, PAIR)], rec_t.at[u, pl.ds(ch * PAIR, PAIR)],
            t_s.at[d, ch], t_r.at[d, ch], (along(d), i),
        )

    for d in range(1, NU):
        give_scale(d).start()
    for ch in range(PARTS):
        for d in range(1, NU):
            give_target(d, ch).start()
    ired[...] = total[...].T * item_scale
    halve_send(0)
    rec_t[u] = snd_t[pl.ds(u * T, T)]
    rec_ts[u] = target_scale

    down = lax.broadcasted_iota(jnp.int32, (NB, NB), 0)
    across = lax.broadcasted_iota(jnp.int32, (NB, NB), 1)
    for k in range(K):
        rows = slice(k * NB, (k + 1) * NB)
        again = slice(EE + k * NB, EE + (k + 1) * NB)
        m = jnp.where(down == across, 1.0, 0.0) - jnp.where(down == near_ref[k : k + 1], 1.0, 0.0)
        side = m.T.astype(jnp.bfloat16)
        back_ref[:, rows] = m.astype(jnp.bfloat16)
        back_ref[:, again] = m.astype(jnp.bfloat16)
        diff_ref[rows, :NB] = side
        diff_ref[rows, NB:] = side
        weight_ref[rows] = jnp.broadcast_to(edge_ref[k : k + 1], (W, NB)).T

    chain = iter(range(LOG + LAST))

    def item_step():
        s = next(chain, None)
        if s is None:
            return
        if s < LOG:
            halve_take(s)
            if s < LAST:
                halve_send(s + 1)
            else:
                double_first()
                double_send(LAST - 1)
        else:
            s = LOG + LAST - 1 - s
            double_take(s)
            if s > 0:
                double_send(s - 1)

    for d in range(1, NU):
        give_dual(d).wait_recv()
        give_step(d).wait_recv()
    for d in range(1, NU):
        give_scale(d).wait_recv()

    GROUP = 128

    def split(x):
        high = x.astype(jnp.bfloat16)
        return high, (x - high.astype(jnp.float32)).astype(jnp.bfloat16)

    def give_result(d, ch):
        device = (along(d), i)
        rows = pl.ds(ch * PAIR, PAIR)
        return (
            send(snd_r.at[along(d), rows], rec_r.at[u, rows], r_s.at[d, ch], r_r.at[d, ch], device),
            send(snd_rs.at[ch], rec_rs.at[u, ch], rs_s.at[d, ch], rs_r.at[d, ch], device),
        )

    def fold(m):
        m = jnp.max(m, axis=0, keepdims=True)
        out = m[:, :W]
        for n in range(1, PAIR):
            out = jnp.maximum(out, m[:, n * W : (n + 1) * W])
        return out

    def own_result(ch):
        rows = pl.ds(ch * PAIR, PAIR)
        return pltpu.make_async_copy(snd_r.at[u, rows], rec_r.at[u, rows], own_m.at[ch])

    def unit(n):
        return n // 2, range(1 + n % 2, NU, 2)

    def unit_start(n):
        ch, ds = unit(n)
        for d in ds:
            for copy in give_result(d, ch):
                copy.start()

    def unit_wait(n):
        ch, ds = unit(n)
        for d in ds:
            for copy in give_result(d, ch):
                copy.wait_recv()

    def sweep_rows(ch, _):
        for d in range(1, NU):
            give_target(d, ch).wait_recv()
        for n in range(PAIR):
            r = ch * PAIR + n
            lanes = slice(n * W, (n + 1) * W)
            for v in range(NU):
                xs[v * B : (v + 1) * B, lanes] = plain(rec_t[v, r], rec_ts[v])
                flux = plain(rec_d[v, r], rec_ds[v])
                for k in range(K):
                    fl[k * NB + v * B : k * NB + (v + 1) * B, lanes] = flux[k * B : (k + 1) * B]

        peaks = None
        for sweep in range(ITERS):
            source = xs[...] if sweep == 0 else ex[...]
            hl[:NB], hl[NB:] = split(source)
            peaks = jnp.zeros((8, PAIR * W), jnp.float32)
            for g in range(0, EE, GROUP):
                rows = slice(g, g + GROUP)
                slope = jnp.dot(diff_ref[rows], hl[...], preferred_element_type=jnp.float32)
                moved = fl[rows] + dual_step * slope
                w = weight_ref[rows]
                parts = []
                for n in range(PAIR):
                    m = moved[:, n * W : (n + 1) * W]
                    square = jnp.sum(m * m, axis=-1, keepdims=True)
                    parts.append(m * (w * lax.rsqrt(jnp.maximum(square, w * w))))
                flux = jnp.concatenate(parts, axis=1) if PAIR > 1 else parts[0]
                fl[rows] = flux
                fhl[rows], fhl[EE + g : EE + g + GROUP] = split(flux)
                peaks = jnp.maximum(peaks, peak(flux))
            div = jnp.dot(back_ref[...], fhl[...], preferred_element_type=jnp.float32)
            target = xs[...]
            if sweep == 0:
                primal = target
            newer = (primal - primal_step * div + primal_step * target) / (1.0 + primal_step)
            if sweep < ITERS - 1:
                ex[...] = 2.0 * newer - primal
            primal = newer

        flux_inverse, flux_scale = steps_of(fold(peaks))
        primal_inverse, primal_scale = steps_of(fold(peak(primal)))
        scales = jnp.concatenate([flux_scale, primal_scale], axis=0)
        snd_rs[ch] = scales
        for n in range(PAIR):
            r = ch * PAIR + n
            lanes = slice(n * W, (n + 1) * W)
            for v in range(NU):
                for k in range(K):
                    part = fl[k * NB + v * B : k * NB + (v + 1) * B, lanes]
                    snd_r[v, r, k * B : (k + 1) * B] = coded(part, flux_inverse)
                snd_r[v, r, E:] = coded(primal[v * B : (v + 1) * B, lanes], primal_inverse)
        own_result(ch).start()
        rec_rs[u, ch] = scales

        for n in range(min(LEAD, 2 * PARTS)):
            @pl.when(ch == n // 2)
            def _():
                if n == 2:
                    item_step()
                unit_start(n)

        return 0

    lax.fori_loop(0, PARTS, sweep_rows, 0)

    for n in range(2 * PARTS):
        unit_wait(n)
        if n % 2 == 0:
            item_step()
        if n + LEAD < 2 * PARTS:
            unit_start(n + LEAD)
    for _ in range(2 * LOG):
        item_step()

    for ch in range(PARTS):
        own_result(ch).wait()
    for q in range(1, NI):
        for c in range(CHUNKS):
            (pass_on(q - 1, c) if q > 1 and q % 2 else gather(q, c)).wait_send()
            for copy in give_user(q, c):
                copy.wait_send()
    for d in range(1, NU):
        for copy in (give_dual(d), give_step(d), give_scale(d)):
            copy.wait_send()
        for ch in range(PARTS):
            give_target(d, ch).wait_send()
            for copy in give_result(d, ch):
                copy.wait_send()
    for s in range(LOG):
        for copy in give_item(s) + (give_all(s) if s < LAST else ()):
            copy.wait_send()


def decode(dims, rec_in, recs_in, gi_in, gis_in, out_p, out_d, out_i, rec_r, rec_rs, gi, gis, op, od, oi, load_m, save_m):
    NU, NI, B, S, K, C, W = dims
    T = S // NU
    PAIR = T // rec_rs.shape[1]
    SEG = C // gis.shape[0]
    parts = [pl.ds(k * B, B) for k in range(K + 1)]
    loads = [
        pltpu.make_async_copy(src, dst, load_m.at[n])
        for n, (src, dst) in enumerate([
            (recs_in, rec_rs), (gis_in, gis), (gi_in, gi),
            *[(rec_in.at[:, :, p], rec_r.at[:, :, p]) for p in parts],
        ])
    ]
    for load in loads:
        load.start()

    def save(n, src, dst):
        copy = pltpu.make_async_copy(src, dst, save_m.at[n])
        copy.start()
        return copy

    def rows_of(g, k, which):
        out = []
        for r in range(g * 8, g * 8 + 8):
            v, t = r // T, r % T
            q = rec_r[v, t, k * B : (k + 1) * B].astype(jnp.int32).astype(jnp.float32)
            out.append(q * rec_rs[v, t // PAIR, which : which + 1])
        return jnp.swapaxes(jnp.stack(out), 0, 1)

    for load in loads[:3]:
        load.wait()
    saves = []
    for n in range(gis.shape[0]):
        rows = slice(n * SEG, (n + 1) * SEG)
        oi[rows] = plain(gi[rows], gis[n])
    saves.append(save(K + 1, oi, out_i))
    for k in range(K):
        loads[3 + k].wait()
        for g in range(S // 8):
            od[:, k, g * 8 : g * 8 + 8] = rows_of(g, k, 0)
        saves.append(save(k, od.at[:, k], out_d.at[:, k]))
    loads[3 + K].wait()
    for g in range(S // 8):
        op[:, g * 8 : g * 8 + 8] = rows_of(g, K, 1)
    saves.append(save(K, op, out_p))
    for copy in saves:
        copy.wait()


def shards(ratings, tile_mask, user_factors, item_factors, neighbours, edge_weight, dual):
    B, S, W = user_factors.shape
    K = neighbours.shape[1]
    NU = lax.axis_size("user")
    NI = lax.axis_size("item")
    C = item_factors.shape[0]
    T = S // NU
    E = B * K
    NB = B * NU
    EE = E * NU
    LOG = NU.bit_length() - 1
    ROWS = B // CHUNKS * S
    PAIR = 2 if T % 2 == 0 else 1
    PARTS = T // PAIR
    dims = (NU, NI, B, S, K, C, W)

    f32, i16, bf16 = jnp.float32, jnp.int16, jnp.bfloat16
    V = pltpu.VMEM
    dma = pltpu.SemaphoreType.DMA
    vmem = pl.BlockSpec(memory_space=pltpu.VMEM)
    hbm = pl.BlockSpec(memory_space=pltpu.HBM)
    scratch = [
        V((tile_mask.shape[1], B), jnp.int32), V((B * S, W), bf16), V((C, W), bf16), V((B, K, S, W), f32),
        V((K, NB), jnp.int32), V((K, NB), f32), dma((5,)), dma((PARTS,)), dma((S // max(T, 8),)), V((B, 1, C), f32), V((EE, 2 * NB), bf16), V((NB, 2 * EE), bf16), V((EE, W), f32),
        V((SLOTS, B // CHUNKS, S, C), bf16), V((NI, B * S, W), bf16), V((CHUNKS, ROWS, W), f32),
        V((CHUNKS, ROWS, W), f32), V((W, C), f32),
        V((NI, CHUNKS, ROWS, W), i16), V((NI, CHUNKS, 8, W), f32),
        V((NI, CHUNKS, ROWS, W), i16), V((NI, CHUNKS, 8, W), f32),
        V((S, E, W), i16), V((S // max(T, 8), 1, W), f32), V((NU, T, E, W), i16), V((NU, 1, W), f32),
        V((B, S, W), f32), V((S, B, W), i16), V((1, W), f32), V((NU, T, B, W), i16), V((NU, 1, W), f32),
        V((NB, PAIR * W), f32), V((NB, PAIR * W), f32), V((2 * NB, PAIR * W), bf16),
        V((EE, PAIR * W), f32), V((2 * EE, PAIR * W), bf16),
        V((NU, T, E + B, W), i16), V((PARTS, 2, W), f32),
        V((C, W), f32), V((LOG, C // 2, W), i16), V((LOG, 8, W), f32),
        V((LOG, C // 2, W), i16), V((LOG, 8, W), f32),
        dma((SLOTS,)),
        *[dma((NI, CHUNKS)) for _ in range(6)],
        *[dma((NU,)) for _ in range(4)], *[dma((NU, PARTS)) for _ in range(2)], *[dma((NU,)) for _ in range(2)],
        *[dma((NU, PARTS)) for _ in range(4)],
        *[dma((LOG,)) for _ in range(8)],
    ]
    held = pl.pallas_call(
        functools.partial(kernel, dims),
        out_shape=(
            jax.ShapeDtypeStruct((NU, T, E + B, W), i16),
            jax.ShapeDtypeStruct((NU, PARTS, 2, W), f32),
            jax.ShapeDtypeStruct((C, W), i16),
            jax.ShapeDtypeStruct((NU // 2, 8, W), f32),
        ),
        in_specs=[hbm] * 7,
        out_specs=[pl.BlockSpec(memory_space=pl.ANY)] + [vmem] * 3,
        scratch_shapes=scratch,
        compiler_params=pltpu.CompilerParams(
            collective_id=0, has_side_effects=True, vmem_limit_bytes=61 << 20
        ),
        cost_estimate=pl.CostEstimate(
            flops=6 * B * S * NI * C * W, bytes_accessed=2 * B * S * NI * C, transcendentals=0
        ),
    )(
        ratings.reshape(B, NI, S, C), tile_mask.T, user_factors.reshape(B * S, W), item_factors,
        dual, neighbours.T, edge_weight.T,
    )
    return pl.pallas_call(
        functools.partial(decode, dims),
        out_shape=(
            jax.ShapeDtypeStruct((B, S, W), f32),
            jax.ShapeDtypeStruct((B, K, S, W), f32),
            jax.ShapeDtypeStruct((C, W), f32),
        ),
        in_specs=[hbm] * 4,
        out_specs=[hbm] * 3,
        scratch_shapes=[
            V((NU, T, E + B, W), i16), V((NU, PARTS, 2, W), f32), V((C, W), i16), V((NU // 2, 8, W), f32),
            V((B, S, W), f32), V((B, K, S, W), f32), V((C, W), f32), dma((K + 4,)), dma((K + 2,)),
        ],
        compiler_params=pltpu.CompilerParams(vmem_limit_bytes=61 << 20),
        cost_estimate=pl.CostEstimate(
            flops=4 * B * (K + 1) * S * W, bytes_accessed=6 * B * (K + 1) * S * W, transcendentals=0
        ),
    )(*held)


def solution(mesh):
    in_specs = (
        P("user", "item"),
        P("user", "item"),
        P("user", "item", None),
        P("item", None),
        P(),
        P(),
        P("user", None, "item", None),
    )
    out_specs = (P("user", "item", None), P("user", None, "item", None), P("item", None))
    return jax.shard_map(shards, mesh=mesh, in_specs=in_specs, out_specs=out_specs, check_vma=False)
```
